32 devices in a mesh: groups: 2 (over y), frames: 4 (over z), heads: 2 (over x), rep: 2 (over core).
Axes of the slice: x: 2, y: 2, z: 4, core: 2. Of those that a mesh axis runs over, the one named last changes fastest.
Arguments:
- query: bfloat16 [4096, 3072], P(('groups', 'frames', 'rep'), 'heads'), parts along dimension 0, may hold values from -120 to 120
- key_proj: bfloat16 [4096, 3072], P(('groups', 'frames', 'rep'), 'heads'), parts along dimension 0, may hold values from -4 to 4
- value: bfloat16 [4096, 3072], P(('groups', 'frames', 'rep'), 'heads'), parts along dimension 0, may hold values from -6 to 6
- block_mask: int32 [24, 8, 8], P('heads'), may hold values from 0 to 1, as said below
- tile_sizes: int32 [2, 4], P('rep'), may hold values from 1 to 128, 256 in all within a row
- temporal_ids: int32 [8], P('heads'), may hold values from 0 to 23, as said below
Outputs:
- attended: bfloat16 [4096, 3072], P(('groups', 'frames', 'rep'), 'heads'), parts along dimension 0
The draws below stay inside these ranges and needn't reach their ends.
There are 2 independent parts, one for each index of `groups`. The reference program is written for one: setup_inputs(seed, part) draws one part's arguments, and reference() takes and returns one part's arrays. A program takes and returns all parts, laid end to end along the dimension named above; an argument that names none is the same for every part. Nothing has to cross between parts.
Inputs may be any that keep to these rules, and one draw needn't show every extreme that they name: `block_mask`: each row of each head's block mask has exactly 4 ones, its diagonal entry among them. Entries j of temporal_ids are distinct and lie in heads (j // 4) * 12 to (j // 4 + 1) * 12 - 1. `tile_sizes`: each row sums to 256, and its largest entry is 128.
All inputs are finite; a program needn't handle non-finite values.
Results may differ from the reference program's by a relative error of at most 0.008.
Values may be sent and summed in bfloat16 or wider, within the bound.
No kernel may reach another device: no remote copies, remote signals or barrier semaphores. Data moves between devices by JAX's collectives and lax.ppermute only.
A program may use at most 64 MiB of HBM per device.

```python
import math
import jax
import jax.numpy as jnp
import numpy as np
from jax import lax

HEADS = 24
HD = 128
TEMP = 8
BLK = 64
HALF = 256
HPD = 12
TPD = 4
WIDTH = 3072
FRAME = 512
NB = 8
LIVE = 4
TILE_MAX = 128
TOKENS = 2048
N_FRAMES = 4
N_REP = 2


def base_keys(key):
    return jnp.clip(jax.random.normal(jax.random.fold_in(key, 7), (TOKENS, WIDTH), jnp.float32), -4.0, 4.0)


def draw_key_proj(key, part):
    keys_drawn = base_keys(key)
    return keys_drawn.astype(jnp.bfloat16)


def draw_query(key, part):
    drawn = jnp.clip(jax.random.normal(jax.random.fold_in(key, 11), (TOKENS, WIDTH), jnp.float32), -4.0, 4.0)
    return drawn.astype(jnp.bfloat16)


def draw_block_mask(key, part):
    ranks_raw = jax.random.randint(key, (HEADS, NB, NB), 0, 1 << 20) * NB + jnp.arange(NB, dtype=jnp.int32)[None, None, :]
    diagonal = jnp.eye(NB, dtype=jnp.int32)[None] == 1
    ranks_raw = jnp.where(diagonal, -1, ranks_raw)
    placing = jnp.argsort(jnp.argsort(ranks_raw, axis=-1), axis=-1)
    return (placing < LIVE).astype(jnp.int32)


def draw_temporal_ids(key, part):
    block_total = TEMP // TPD
    split_keys = jax.random.split(key, block_total)
    picks = jax.vmap(lambda one_key: jax.random.permutation(one_key, HPD)[:TPD])(split_keys)
    offsets = jnp.arange(block_total, dtype=jnp.int32)[:, None] * HPD
    return (picks.astype(jnp.int32) + offsets).reshape(TEMP).astype(jnp.int32)


def levels(stream_key, extent, cuts, low, largest):
    loudness, own = 1.0, jax.random.fold_in(stream_key, 6)
    for dim, blocks in cuts:
        heights = jnp.exp(jax.random.uniform(jax.random.fold_in(own, dim), (blocks,), jnp.float32, low / len(cuts), largest / len(cuts)))
        loudness = loudness * jnp.repeat(heights, extent[dim] // blocks).reshape([-1 if axis == dim else 1 for axis in range(len(extent))])
    return loudness


def length_profile(amount, total, bound, lean):
    loads = [(1 << 20) // math.isqrt(standing ** lean) + 1 for standing in range(2, amount + 1)]
    surplus, counts = total - bound - (amount - 1), [1] * (amount - 1)
    while surplus > 0:
        candidates = [i for i in range(amount - 1) if counts[i] < bound]
        mass, remaining = sum([loads[i] for i in candidates]), surplus
        for i in candidates:
            more = min(bound - counts[i], max(1, remaining * loads[i] // mass), surplus)
            counts[i] = counts[i] + more
            surplus = surplus - more
    return np.array([bound] + counts)


def ragged_sizes(stream_key, amount, total, most, lean):
    if amount == 2:
        one = jax.random.randint(stream_key, (), max(1, total - most), min(most, total - 1) + 1)
        return jnp.stack([one, total - one])
    lengths = jnp.asarray(length_profile(amount, total, most, lean), jnp.int32)
    twos = (amount - 1) // 2
    source_of, receiver = lengths[1:1 + 2 * twos:2], lengths[2:2 + 2 * twos:2]
    room = jnp.minimum(source_of - 1, most - receiver)
    shifted = jax.random.randint(jax.random.fold_in(stream_key, 1), (twos,), 0, 1 << 20) % (room + 1)
    lengths = lengths.at[1:1 + 2 * twos:2].set(source_of - shifted).at[2:2 + 2 * twos:2].set(receiver + shifted)
    return lengths[jax.random.permutation(jax.random.fold_in(stream_key, 2), amount)]


def noise(stream_key, dims, scale, reach, cuts=(), held_as=jnp.bfloat16):
    values = scale * jax.random.normal(stream_key, dims, jnp.float32)
    if cuts:
        values = values * levels(stream_key, dims, cuts, -0.22, 0.18)
    return jnp.clip(values, -reach, reach).astype(held_as)


def setup_inputs(seed: int = 0, part: int = 0) -> dict:
    seeds = jax.random.split(jax.random.key(seed), 7)
    part_splits = jax.random.split(jax.random.fold_in(seeds[6], part), 7)
    query = draw_query(jax.random.fold_in(jax.random.fold_in(seeds[6], part), 71), part)
    key_proj = draw_key_proj(jax.random.fold_in(jax.random.fold_in(seeds[6], part), 71), part)
    value = noise(part_splits[2], (TOKENS, WIDTH), 1.0, 6.0, ((0, 8), (1, 2)))
    block_mask = draw_block_mask(jax.random.fold_in(seeds[6], 71), part)
    tile_sizes = jax.vmap(lambda own: ragged_sizes(own, N_FRAMES, HALF, TILE_MAX, 2))(jax.random.split(seeds[4], N_REP)).reshape((N_REP, N_FRAMES)).astype(jnp.int32)
    temporal_ids = draw_temporal_ids(jax.random.fold_in(seeds[6], 71), part)
    return {"query": query, "key_proj": key_proj, "value": value, "block_mask": block_mask, "tile_sizes": tile_sizes, "temporal_ids": temporal_ids}


MASKED_SCORE = -1e30


def softmax_weights(scores):
    highest = jnp.max(scores, axis=-1, keepdims=True)
    raised = jnp.exp(scores - highest)
    return (raised / jnp.sum(raised, axis=-1, keepdims=True)).astype(jnp.bfloat16)


def reference(query, key_proj, value, block_mask, tile_sizes, temporal_ids):
    score_scale = HD ** -0.5

    def by_heads(array):
        return array.reshape(N_FRAMES, FRAME, HEADS, HD).transpose(2, 0, 1, 3)

    head_query = by_heads(query)
    head_keys = by_heads(key_proj)
    head_values = by_heads(value)

    def spatial_head(head_args):
        one_query, one_keys, one_values, one_mask = head_args
        scores = jnp.einsum("fad,fbd->fab", one_query.astype(jnp.float32), one_keys.astype(jnp.float32)) * score_scale
        allowed = jnp.repeat(jnp.repeat(one_mask, BLK, axis=0), BLK, axis=1) == 1
        scores = jnp.where(allowed[None], scores, MASKED_SCORE)
        weights = softmax_weights(scores)
        return jnp.einsum("fab,fbd->fad", weights.astype(jnp.float32), one_values.astype(jnp.float32)).astype(jnp.bfloat16)

    spatial_out = lax.map(spatial_head, (head_query, head_keys, head_values, block_mask))

    temp_query = head_query[temporal_ids]
    temp_keys = head_keys[temporal_ids]
    temp_values = head_values[temporal_ids]
    temp_out = jnp.zeros((TEMP, N_FRAMES, FRAME, HD), jnp.bfloat16)
    slot_index = jnp.arange(TILE_MAX, dtype=jnp.int32)
    for half_index in range(N_REP):
        tile_len = tile_sizes[half_index].astype(jnp.int32)
        starts = jnp.cumsum(tile_len).astype(jnp.int32) - tile_len
        positions = half_index * HALF + starts[:, None] + slot_index[None, :]
        live_slots = slot_index[None, :] < tile_len[:, None]
        safe_rows = jnp.minimum(positions, FRAME - 1).astype(jnp.int32)

        def temporal_tile(tile_args):
            rows_here, live_here = tile_args
            tile_query = temp_query[:, :, rows_here, :].reshape(TEMP, N_FRAMES * TILE_MAX, HD)
            tile_keys = temp_keys[:, :, rows_here, :].reshape(TEMP, N_FRAMES * TILE_MAX, HD)
            tile_values = temp_values[:, :, rows_here, :].reshape(TEMP, N_FRAMES * TILE_MAX, HD)
            key_live = jnp.tile(live_here, N_FRAMES)
            scores = jnp.einsum("hqd,hkd->hqk", tile_query.astype(jnp.float32), tile_keys.astype(jnp.float32)) * score_scale
            scores = jnp.where(key_live[None, None, :], scores, MASKED_SCORE)
            weights = softmax_weights(scores)
            tile_out = jnp.einsum("hqk,hkd->hqd", weights.astype(jnp.float32), tile_values.astype(jnp.float32)).astype(jnp.bfloat16)
            return tile_out.reshape(TEMP, N_FRAMES, TILE_MAX, HD)

        tile_out = lax.map(temporal_tile, (safe_rows, live_slots))
        target = jnp.where(live_slots, positions, FRAME).reshape(-1).astype(jnp.int32)
        placed = tile_out.transpose(1, 2, 0, 3, 4).reshape(TEMP, N_FRAMES, N_FRAMES * TILE_MAX, HD)
        temp_out = temp_out.at[:, :, target, :].set(placed, mode="drop")

    all_out = spatial_out.at[temporal_ids].set(temp_out)
    return all_out.transpose(1, 2, 0, 3).reshape(TOKENS, WIDTH)
```

```python
import math

import jax
import jax.numpy as jnp
from jax import lax
from jax.experimental import pallas as pl
from jax.experimental.pallas import tpu as pltpu
from jax.sharding import PartitionSpec as P

HD = 128
BLK = 64


MASKED_SCORE = -1e30


def softmax_weights(scores):
    highest = jnp.max(scores, axis=-1, keepdims=True)
    raised = jnp.exp(scores - highest)
    return (raised / jnp.sum(raised, axis=-1, keepdims=True)).astype(jnp.bfloat16)


def select_heads(token_rows, picker):
    head_grid = token_rows.reshape(token_rows.shape[0], -1, HD)
    chosen = jnp.einsum(
        "rhd,th->rtd", head_grid, picker.astype(jnp.bfloat16), preferred_element_type=jnp.float32
    )
    return chosen.astype(jnp.bfloat16)


def spread_heads(head_grid, picker):
    return jnp.einsum(
        "rtd,th->rhd", head_grid, picker.astype(jnp.bfloat16), preferred_element_type=jnp.float32
    )


def local_by_tile(query, key_proj, value, block_mask, tile_sizes, temporal_ids):
    half_rows = query.shape[0]
    heads_here = block_mask.shape[0]
    temp_here = temporal_ids.shape[0]
    spat_here = heads_here - temp_here
    frame_blocks = block_mask.shape[1]
    frame_count = lax.axis_size("frames")
    slot_count = 2 * half_rows // frame_count
    score_scale = HD ** (-0.5)
    local_ids = temporal_ids - lax.axis_index("heads") * heads_here
    head_range = jnp.arange(heads_here, dtype=jnp.int32)
    pick_temp = local_ids[:, None] == head_range[None, :]
    temp_flag = jnp.sum(pick_temp.astype(jnp.int32), axis=0)
    spat_rank = jnp.cumsum(1 - temp_flag) - 1
    pick_spat = (spat_rank[None, :] == jnp.arange(spat_here, dtype=jnp.int32)[:, None]) & (
        temp_flag[None, :] == 0
    )
    tile_len = tile_sizes[0]
    starts = jnp.cumsum(tile_len) - tile_len
    slot_index = jnp.arange(slot_count, dtype=jnp.int32)
    source_rows = jnp.minimum(starts[:, None] + slot_index[None, :], half_rows - 1)
    frame_range = jnp.arange(frame_count, dtype=jnp.int32)
    own_len = jnp.sum(jnp.where(frame_range == lax.axis_index("frames"), tile_len, 0))
    key_live = jnp.tile(slot_index < own_len, frame_count)
    send_query = select_heads(query, pick_temp)[source_rows]
    send_keys = select_heads(key_proj, pick_temp)[source_rows]
    send_values = select_heads(value, pick_temp)[source_rows]
    tile_query = lax.all_to_all(send_query, "frames", split_axis=0, concat_axis=0, tiled=True)
    tile_keys = lax.all_to_all(send_keys, "frames", split_axis=0, concat_axis=0, tiled=True)
    tile_values = lax.all_to_all(send_values, "frames", split_axis=0, concat_axis=0, tiled=True)
    item_count = tile_query.shape[2]
    flat_query = tile_query.reshape(frame_count * slot_count, item_count, HD)
    flat_keys = tile_keys.reshape(frame_count * slot_count, item_count, HD)
    flat_values = tile_values.reshape(frame_count * slot_count, item_count, HD)
    scores = (
        jnp.einsum("qhd,khd->hqk", flat_query, flat_keys, preferred_element_type=jnp.float32)
        * score_scale
    )
    scores = jnp.where(key_live[None, None, :], scores, MASKED_SCORE)
    weights = softmax_weights(scores)
    tile_out = jnp.einsum(
        "hqk,khd->qhd", weights, flat_values, preferred_element_type=jnp.float32
    ).astype(jnp.bfloat16)
    returned = lax.all_to_all(
        tile_out.reshape(frame_count, slot_count, item_count, HD),
        "frames",
        split_axis=0,
        concat_axis=0,
        tiled=True,
    )
    own_keys = select_heads(key_proj, pick_spat)
    own_values = select_heads(value, pick_spat)
    spat_keys, spat_values = (
        lax.all_gather(own_keys, "rep", axis=0, tiled=True),
        lax.all_gather(own_values, "rep", axis=0, tiled=True),
    )
    spat_query = select_heads(query, pick_spat)
    spat_mask = (
        jnp.einsum("hij,th->tij", block_mask.astype(jnp.float32), pick_spat.astype(jnp.float32))
        > 0.5
    )
    query_blocks = half_rows // BLK
    mask_rows = lax.dynamic_slice_in_dim(
        spat_mask, lax.axis_index("rep") * query_blocks, query_blocks, 1
    )
    scores = (
        jnp.einsum("qhd,khd->hqk", spat_query, spat_keys, preferred_element_type=jnp.float32)
        * score_scale
    )
    shaped = scores.reshape(spat_here, query_blocks, BLK, frame_blocks, BLK)
    shaped = jnp.where(mask_rows[:, :, None, :, None], shaped, MASKED_SCORE)
    weights = softmax_weights(shaped.reshape(spat_here, half_rows, frame_blocks * BLK))
    spat_out = jnp.einsum(
        "hqk,khd->qhd", weights, spat_values, preferred_element_type=jnp.float32
    ).astype(jnp.bfloat16)
    positions = jnp.arange(half_rows, dtype=jnp.int32)
    tile_ends = starts + tile_len
    tile_of = jnp.sum((positions[:, None] >= tile_ends[None, :]).astype(jnp.int32), axis=1)
    picked_start = jnp.sum(
        jnp.where(tile_of[:, None] == frame_range[None, :], starts[None, :], 0), axis=1
    )
    flat_index = tile_of * slot_count + positions - picked_start
    temp_out = returned.reshape(frame_count * slot_count, temp_here, HD)[flat_index]
    combined = spread_heads(spat_out, pick_spat) + spread_heads(temp_out, pick_temp)
    return combined.astype(jnp.bfloat16).reshape(half_rows, heads_here * HD)


EXP2_SCALE = HD ** -0.5 * math.log2(math.e)
ANY = pl.BlockSpec(memory_space=pl.ANY)
SMEM = pl.BlockSpec(memory_space=pltpu.SMEM)
VMEM = pl.BlockSpec(memory_space=pltpu.VMEM)


def scores_of(rows, keys):
    return lax.dot_general(rows, keys, (((1,), (1,)), ((), ())), preferred_element_type=jnp.float32)


def attend(scores, values):
    highest = scores[0].max(axis=-1, keepdims=True)
    for more in scores[1:]:
        highest = jnp.maximum(highest, more.max(axis=-1, keepdims=True))
    total, out = 0.0, 0.0
    for group, group_values in zip(scores, values):
        raised = jnp.exp2((group - highest) * EXP2_SCALE)
        total = total + raised.sum(axis=-1, keepdims=True)
        out = out + jnp.dot(raised.astype(jnp.bfloat16), group_values, preferred_element_type=jnp.float32)
    return (out / total).astype(jnp.bfloat16)


def columns(index):
    return pl.ds(pl.multiple_of(index * HD, HD), HD)


def head_of(ids_ref, slot, heads_here):
    return lax.rem(ids_ref[slot], heads_here)


def pack_kernel(frames, heads_here, parts, where_ref, ids_ref, query, key_proj, value, *rest):
    outs, sems = rest[:-1], rest[-1]
    sources = {"q": query, "k": key_proj, "v": value}
    copies = []
    for out, (mask, names) in zip(outs, parts):
        head = head_of(ids_ref, where_ref[0] ^ mask, heads_here)
        for place, name in enumerate(names):
            copies.append(
                pltpu.make_async_copy(
                    sources[name].at[:, columns(head)],
                    out.at[:, place * HD : (place + 1) * HD],
                    sems.at[len(copies)],
                )
            )
            copies[-1].start()
    for copy in copies:
        copy.wait()


def pack(where, ids, query, key_proj, value, parts, frames, heads_here):
    rows = query.shape[0]
    count = sum(len(names) for _, names in parts)
    return pl.pallas_call(
        lambda *refs: pack_kernel(frames, heads_here, parts, *refs),
        out_shape=[jax.ShapeDtypeStruct((rows, len(names) * HD), query.dtype) for _, names in parts],
        in_specs=[SMEM, SMEM, ANY, ANY, ANY],
        out_specs=[ANY] * len(parts),
        scratch_shapes=[pltpu.SemaphoreType.DMA((count,))],
        name="pack",
        compiler_params=pltpu.CompilerParams(vmem_limit_bytes=4 << 20),
        cost_estimate=pl.CostEstimate(flops=0, bytes_accessed=2 * count * rows * HD * 2, transcendentals=0),
    )(where, ids, query, key_proj, value)


def spatial_kernel(step_heads, heads_here, where_ref, ids_ref, mask_ref, query, key_own, key_other, value_own, value_other, out):
    rows = query.shape[0]
    own_blocks, frame_blocks = rows // BLK, mask_ref.shape[-1]
    rep = where_ref[1]
    block = lax.broadcasted_iota(jnp.int32, (frame_blocks, 2 * rows), 1) // BLK
    block = lax.rem(block + rep * own_blocks, frame_blocks)
    spread = (block == lax.broadcasted_iota(jnp.int32, block.shape, 0)).astype(jnp.float32)
    for item in range(step_heads):
        here = pl.program_id(0) * step_heads + item
        temporal = head_of(ids_ref, 0, heads_here) == here
        for slot in range(1, ids_ref.shape[0]):
            temporal |= head_of(ids_ref, slot, heads_here) == here

        @pl.when(jnp.logical_not(temporal))
        def _():
            part = slice(item * HD, (item + 1) * HD)
            seen = jnp.dot(mask_ref[item].astype(jnp.float32), spread, preferred_element_type=jnp.float32)
            seen = jnp.where(rep == 0, seen[:own_blocks], seen[own_blocks:])
            bias = jnp.where(seen > 0.5, 0.0, MASKED_SCORE)
            bias = jnp.broadcast_to(bias[:, None, :], (own_blocks, BLK, 2 * rows)).reshape(rows, 2 * rows)
            own = scores_of(query[:, part], key_own[:, part]) + bias[:, :rows]
            other = scores_of(query[:, part], key_other[:, part]) + bias[:, rows:]
            out[:, part] = attend([own, other], [value_own[:, part], value_other[:, part]])


def spatial(where, ids, mask, query, key_own, key_other, value_own, value_other, step_heads=2):
    rows, width = query.shape
    heads_here, blocks = width // HD, mask.shape[-1]
    piece = pl.BlockSpec((rows, step_heads * HD), lambda i: (0, i))
    return pl.pallas_call(
        lambda *refs: spatial_kernel(step_heads, heads_here, *refs),
        out_shape=jax.ShapeDtypeStruct((rows, width), query.dtype),
        grid=(heads_here // step_heads,),
        in_specs=[SMEM, SMEM, pl.BlockSpec((step_heads, blocks, blocks), lambda i: (i, 0, 0))] + [piece] * 5,
        out_specs=piece,
        name="spatial",
        compiler_params=pltpu.CompilerParams(vmem_limit_bytes=24 << 20),
        cost_estimate=pl.CostEstimate(
            flops=8 * rows * rows * width, bytes_accessed=12 * rows * width, transcendentals=2 * rows * rows * heads_here
        ),
    )(where, ids, mask, query, key_own, key_other, value_own, value_other)


def tile_bias(sizes_ref, rows):
    down = lax.broadcasted_iota(jnp.int32, (rows, 1), 0)
    across = lax.broadcasted_iota(jnp.int32, (1, rows), 1)
    tile_down, tile_across, end = jnp.zeros_like(down), jnp.zeros_like(across), 0
    for tile in range(sizes_ref.shape[1]):
        end = end + sizes_ref[0, tile]
        tile_down = tile_down + (down >= end).astype(jnp.int32)
        tile_across = tile_across + (across >= end).astype(jnp.int32)
    return jnp.where(tile_down == tile_across, 0.0, MASKED_SCORE)


def temporal_kernel(heads_here, where_ref, ids_ref, sizes_ref, query, key_proj, value, *rest):
    partners = len(rest) // 2 - 1
    received, outs, own, sems = rest[:partners], rest[partners : 2 * partners + 1], rest[-2], rest[-1]
    rows = query.shape[0]
    head = head_of(ids_ref, where_ref[0], heads_here)
    copies = [
        pltpu.make_async_copy(source.at[:, columns(head)], own.at[:, i * HD : (i + 1) * HD], sems.at[i])
        for i, source in enumerate((query, key_proj, value))
    ]
    for copy in copies:
        copy.start()
    bias = tile_bias(sizes_ref, rows)
    for copy in copies:
        copy.wait()
    pieces = (own,) + tuple(received)
    keys = [piece[:, HD : 2 * HD] for piece in pieces]
    values = [piece[:, 2 * HD :] for piece in pieces]
    for piece, out in zip(pieces, outs):
        out[...] = attend([scores_of(piece[:, :HD], group) + bias for group in keys], values)


def temporal(where, ids, sizes, query, key_proj, value, received):
    rows, width = query.shape
    frames = len(received) + 1
    return pl.pallas_call(
        lambda *refs: temporal_kernel(width // HD, *refs),
        out_shape=[jax.ShapeDtypeStruct((rows, HD), query.dtype)] * frames,
        in_specs=[SMEM] * 3 + [ANY] * 3 + [VMEM] * len(received),
        out_specs=[VMEM] * frames,
        scratch_shapes=[pltpu.VMEM((rows, 3 * HD), query.dtype), pltpu.SemaphoreType.DMA((3,))],
        name="temporal",
        compiler_params=pltpu.CompilerParams(vmem_limit_bytes=24 << 20),
        cost_estimate=pl.CostEstimate(
            flops=4 * (frames * rows) ** 2 * HD, bytes_accessed=8 * frames * rows * HD, transcendentals=(frames * rows) ** 2
        ),
    )(where, ids, sizes, query, key_proj, value, *received)


def merge_kernel(heads_here, where_ref, ids_ref, given, *rest):
    pieces, out, sems = rest[:-2], rest[-2], rest[-1]
    copies = []
    for mask, piece in enumerate(pieces):
        head = head_of(ids_ref, where_ref[0] ^ mask, heads_here)
        copies.append(pltpu.make_async_copy(piece, out.at[:, columns(head)], sems.at[mask]))
        copies[-1].start()
    for copy in copies:
        copy.wait()


def merge(where, ids, out, pieces):
    rows, width = out.shape
    return pl.pallas_call(
        lambda *refs: merge_kernel(width // HD, *refs),
        out_shape=jax.ShapeDtypeStruct(out.shape, out.dtype),
        in_specs=[SMEM, SMEM, ANY] + [VMEM] * len(pieces),
        out_specs=ANY,
        scratch_shapes=[pltpu.SemaphoreType.DMA((len(pieces),))],
        input_output_aliases={2: 0},
        name="merge",
        compiler_params=pltpu.CompilerParams(vmem_limit_bytes=4 << 20),
        cost_estimate=pl.CostEstimate(flops=0, bytes_accessed=4 * len(pieces) * rows * HD, transcendentals=0),
    )(where, ids, out, *pieces)


def local_by_head(query, key_proj, value, block_mask, tile_sizes, temporal_ids):
    frames = lax.axis_size("frames")
    heads_here = block_mask.shape[0]
    where = jnp.stack([lax.axis_index("frames"), lax.axis_index("rep")]).astype(jnp.int32)

    def exchange(array, mask):
        return lax.ppermute(array, "frames", [(i, i ^ mask) for i in range(frames)])

    def swap(array):
        return lax.ppermute(array, "rep", [(0, 1), (1, 0)])

    masks = list(range(1, frames))
    packed = pack(where, temporal_ids, query, key_proj, value, [(m, "qkv") for m in masks], frames, heads_here)
    received = [exchange(piece, m) for piece, m in zip(packed, masks)]
    keys_sent, values_sent, *_ = lax.optimization_barrier((key_proj, value, *packed))
    key_other, value_other = swap(keys_sent), swap(values_sent)
    out = spatial(where, temporal_ids, block_mask, query, key_proj, key_other, value, value_other)
    out, *received = lax.optimization_barrier((out, *received))
    pieces = temporal(where, temporal_ids, tile_sizes, query, key_proj, value, received)
    returned = [pieces[0]] + [exchange(piece, m) for piece, m in zip(pieces[1:], masks)]
    return merge(where, temporal_ids, out, returned)


def local(query, key_proj, value, block_mask, tile_sizes, temporal_ids):
    frames, reps = lax.axis_size("frames"), lax.axis_size("rep")
    by_head = temporal_ids.shape[0] == frames and frames & (frames - 1) == 0 and reps == 2
    form = local_by_head if by_head else local_by_tile
    return form(query, key_proj, value, block_mask, tile_sizes, temporal_ids)


def solution(mesh):
    in_specs = (
        P(("groups", "frames", "rep"), "heads"),
        P(("groups", "frames", "rep"), "heads"),
        P(("groups", "frames", "rep"), "heads"),
        P("heads", None, None),
        P("rep", None),
        P("heads"),
    )
    out_specs = P(("groups", "frames", "rep"), "heads")
    return jax.shard_map(local, mesh=mesh, in_specs=in_specs, out_specs=out_specs, check_vma=False)
```

```python
import math

import jax
import jax.numpy as jnp
from jax import lax
from jax.experimental import pallas as pl
from jax.experimental.pallas import tpu as pltpu
from jax.sharding import PartitionSpec as P


HD = 128
BLK = 64


MASKED_SCORE = -1e30


def softmax_weights(scores):
    highest = jnp.max(scores, axis=-1, keepdims=True)
    raised = jnp.exp(scores - highest)
    return (raised / jnp.sum(raised, axis=-1, keepdims=True)).astype(jnp.bfloat16)


def select_heads(token_rows, picker):
    head_grid = token_rows.reshape(token_rows.shape[0], -1, HD)
    chosen = jnp.einsum(
        "rhd,th->rtd", head_grid, picker.astype(jnp.bfloat16), preferred_element_type=jnp.float32
    )
    return chosen.astype(jnp.bfloat16)


def spread_heads(head_grid, picker):
    return jnp.einsum(
        "rtd,th->rhd", head_grid, picker.astype(jnp.bfloat16), preferred_element_type=jnp.float32
    )


def local_by_tile(query, key_proj, value, block_mask, tile_sizes, temporal_ids):
    half_rows = query.shape[0]
    heads_here = block_mask.shape[0]
    temp_here = temporal_ids.shape[0]
    spat_here = heads_here - temp_here
    frame_blocks = block_mask.shape[1]
    frame_count = lax.axis_size("frames")
    slot_count = 2 * half_rows // frame_count
    score_scale = HD ** (-0.5)
    local_ids = temporal_ids - lax.axis_index("heads") * heads_here
    head_range = jnp.arange(heads_here, dtype=jnp.int32)
    pick_temp = local_ids[:, None] == head_range[None, :]
    temp_flag = jnp.sum(pick_temp.astype(jnp.int32), axis=0)
    spat_rank = jnp.cumsum(1 - temp_flag) - 1
    pick_spat = (spat_rank[None, :] == jnp.arange(spat_here, dtype=jnp.int32)[:, None]) & (
        temp_flag[None, :] == 0
    )
    tile_len = tile_sizes[0]
    starts = jnp.cumsum(tile_len) - tile_len
    slot_index = jnp.arange(slot_count, dtype=jnp.int32)
    source_rows = jnp.minimum(starts[:, None] + slot_index[None, :], half_rows - 1)
    frame_range = jnp.arange(frame_count, dtype=jnp.int32)
    own_len = jnp.sum(jnp.where(frame_range == lax.axis_index("frames"), tile_len, 0))
    key_live = jnp.tile(slot_index < own_len, frame_count)
    send_query = select_heads(query, pick_temp)[source_rows]
    send_keys = select_heads(key_proj, pick_temp)[source_rows]
    send_values = select_heads(value, pick_temp)[source_rows]
    tile_query = lax.all_to_all(send_query, "frames", split_axis=0, concat_axis=0, tiled=True)
    tile_keys = lax.all_to_all(send_keys, "frames", split_axis=0, concat_axis=0, tiled=True)
    tile_values = lax.all_to_all(send_values, "frames", split_axis=0, concat_axis=0, tiled=True)
    item_count = tile_query.shape[2]
    flat_query = tile_query.reshape(frame_count * slot_count, item_count, HD)
    flat_keys = tile_keys.reshape(frame_count * slot_count, item_count, HD)
    flat_values = tile_values.reshape(frame_count * slot_count, item_count, HD)
    scores = (
        jnp.einsum("qhd,khd->hqk", flat_query, flat_keys, preferred_element_type=jnp.float32)
        * score_scale
    )
    scores = jnp.where(key_live[None, None, :], scores, MASKED_SCORE)
    weights = softmax_weights(scores)
    tile_out = jnp.einsum(
        "hqk,khd->qhd", weights, flat_values, preferred_element_type=jnp.float32
    ).astype(jnp.bfloat16)
    returned = lax.all_to_all(
        tile_out.reshape(frame_count, slot_count, item_count, HD),
        "frames",
        split_axis=0,
        concat_axis=0,
        tiled=True,
    )
    own_keys = select_heads(key_proj, pick_spat)
    own_values = select_heads(value, pick_spat)
    spat_keys, spat_values = (
        lax.all_gather(own_keys, "rep", axis=0, tiled=True),
        lax.all_gather(own_values, "rep", axis=0, tiled=True),
    )
    spat_query = select_heads(query, pick_spat)
    spat_mask = (
        jnp.einsum("hij,th->tij", block_mask.astype(jnp.float32), pick_spat.astype(jnp.float32))
        > 0.5
    )
    query_blocks = half_rows // BLK
    mask_rows = lax.dynamic_slice_in_dim(
        spat_mask, lax.axis_index("rep") * query_blocks, query_blocks, 1
    )
    scores = (
        jnp.einsum("qhd,khd->hqk", spat_query, spat_keys, preferred_element_type=jnp.float32)
        * score_scale
    )
    shaped = scores.reshape(spat_here, query_blocks, BLK, frame_blocks, BLK)
    shaped = jnp.where(mask_rows[:, :, None, :, None], shaped, MASKED_SCORE)
    weights = softmax_weights(shaped.reshape(spat_here, half_rows, frame_blocks * BLK))
    spat_out = jnp.einsum(
        "hqk,khd->qhd", weights, spat_values, preferred_element_type=jnp.float32
    ).astype(jnp.bfloat16)
    positions = jnp.arange(half_rows, dtype=jnp.int32)
    tile_ends = starts + tile_len
    tile_of = jnp.sum((positions[:, None] >= tile_ends[None, :]).astype(jnp.int32), axis=1)
    picked_start = jnp.sum(
        jnp.where(tile_of[:, None] == frame_range[None, :], starts[None, :], 0), axis=1
    )
    flat_index = tile_of * slot_count + positions - picked_start
    temp_out = returned.reshape(frame_count * slot_count, temp_here, HD)[flat_index]
    combined = spread_heads(spat_out, pick_spat) + spread_heads(temp_out, pick_temp)
    return combined.astype(jnp.bfloat16).reshape(half_rows, heads_here * HD)


EXP2_SCALE = HD ** -0.5 * math.log2(math.e)
HBM = pl.BlockSpec(memory_space=pltpu.HBM)
ANY = pl.BlockSpec(memory_space=pl.ANY)
SMEM = pl.BlockSpec(memory_space=pltpu.SMEM)
VMEM = pl.BlockSpec(memory_space=pltpu.VMEM)


def scores_of(rows, keys):
    return lax.dot_general(rows, keys, (((1,), (1,)), ((), ())), preferred_element_type=jnp.float32)


def attend(scores, values):
    highest = scores[0].max(axis=-1, keepdims=True)
    for more in scores[1:]:
        highest = jnp.maximum(highest, more.max(axis=-1, keepdims=True))
    total, out = 0.0, 0.0
    for group, group_values in zip(scores, values):
        raised = jnp.exp2((group - highest) * EXP2_SCALE)
        total = total + raised.sum(axis=-1, keepdims=True)
        out = out + jnp.dot(raised.astype(jnp.bfloat16), group_values, preferred_element_type=jnp.float32)
    return (out / total).astype(jnp.bfloat16)


def columns(index):
    return pl.ds(pl.multiple_of(index * HD, HD), HD)


def head_of(ids_ref, slot, heads_here):
    return lax.rem(ids_ref[slot], heads_here)


def pack_kernel(heads_here, parts, ids_hbm, query, key_proj, value, *rest):
    outs, ids_ref, sems = rest[: len(parts)], rest[-2], rest[-1]
    sources = {"q": query, "k": key_proj, "v": value}
    fetch = pltpu.make_async_copy(ids_hbm, ids_ref, sems.at[0])
    fetch.start()
    frame = lax.axis_index("frames")
    fetch.wait()
    copies = []
    for out, (mask, names) in zip(outs, parts):
        head = head_of(ids_ref, frame ^ mask, heads_here)
        for place, name in enumerate(names):
            copies.append(
                pltpu.make_async_copy(
                    sources[name].at[:, columns(head)],
                    out.at[:, place * HD : (place + 1) * HD],
                    sems.at[len(copies) + 1],
                )
            )
            copies[-1].start()
    for copy in copies:
        copy.wait()


def pack(ids, query, key_proj, value, parts, heads_here):
    rows = query.shape[0]
    count = sum(len(names) for _, names in parts)
    return pl.pallas_call(
        lambda *refs: pack_kernel(heads_here, parts, *refs),
        out_shape=[pltpu.VMEM((rows, len(names) * HD), query.dtype) for _, names in parts],
        in_specs=[HBM] * 4,
        out_specs=[VMEM] * len(parts),
        scratch_shapes=[pltpu.SMEM(ids.shape, jnp.int32), pltpu.SemaphoreType.DMA((count + 1,))],
        name="pack",
        compiler_params=pltpu.CompilerParams(vmem_limit_bytes=4 << 20),
        cost_estimate=pl.CostEstimate(flops=0, bytes_accessed=4 * count * rows * HD, transcendentals=0),
    )(*(pltpu.with_memory_space_constraint(array, pltpu.HBM) for array in (ids, query, key_proj, value)))


def spatial_kernel(step_heads, heads_here, where_ref, ids_ref, mask_ref, query, key_own, key_other, value_own, value_other, out):
    rows = query.shape[0]
    own_blocks, frame_blocks = rows // BLK, mask_ref.shape[-1]
    rep = where_ref[1]
    block = lax.broadcasted_iota(jnp.int32, (frame_blocks, 2 * rows), 1) // BLK
    block = lax.rem(block + rep * own_blocks, frame_blocks)
    spread = (block == lax.broadcasted_iota(jnp.int32, block.shape, 0)).astype(jnp.float32)
    for item in range(step_heads):
        here = pl.program_id(0) * step_heads + item
        temporal = head_of(ids_ref, 0, heads_here) == here
        for slot in range(1, ids_ref.shape[0]):
            temporal |= head_of(ids_ref, slot, heads_here) == here

        @pl.when(jnp.logical_not(temporal))
        def _():
            part = slice(item * HD, (item + 1) * HD)
            seen = jnp.dot(mask_ref[item].astype(jnp.float32), spread, preferred_element_type=jnp.float32)
            seen = jnp.where(rep == 0, seen[:own_blocks], seen[own_blocks:])
            bias = jnp.where(seen > 0.5, 0.0, MASKED_SCORE)
            bias = jnp.broadcast_to(bias[:, None, :], (own_blocks, BLK, 2 * rows)).reshape(rows, 2 * rows)
            own = scores_of(query[:, part], key_own[:, part]) + bias[:, :rows]
            other = scores_of(query[:, part], key_other[:, part]) + bias[:, rows:]
            out[:, part] = attend([own, other], [value_own[:, part], value_other[:, part]])


def spatial(where, ids, mask, query, key_own, key_other, value_own, value_other, step_heads=2):
    rows, width = query.shape
    heads_here, blocks = width // HD, mask.shape[-1]
    piece = pl.BlockSpec((rows, step_heads * HD), lambda i: (0, i))
    return pl.pallas_call(
        lambda *refs: spatial_kernel(step_heads, heads_here, *refs),
        out_shape=jax.ShapeDtypeStruct((rows, width), query.dtype),
        grid=(heads_here // step_heads,),
        in_specs=[SMEM, SMEM, pl.BlockSpec((step_heads, blocks, blocks), lambda i: (i, 0, 0))] + [piece] * 5,
        out_specs=piece,
        name="spatial",
        compiler_params=pltpu.CompilerParams(vmem_limit_bytes=24 << 20),
        cost_estimate=pl.CostEstimate(
            flops=8 * rows * rows * width, bytes_accessed=12 * rows * width, transcendentals=2 * rows * rows * heads_here
        ),
    )(where, ids, mask, query, key_own, key_other, value_own, value_other)


def tile_bias_kernel(sizes_ref, out):
    rows = out.shape[0]
    down = lax.broadcasted_iota(jnp.int32, (rows, 1), 0)
    across = lax.broadcasted_iota(jnp.int32, (1, rows), 1)
    tile_down, tile_across, end = jnp.zeros_like(down), jnp.zeros_like(across), 0
    for tile in range(sizes_ref.shape[1]):
        end = end + sizes_ref[0, tile]
        tile_down = tile_down + (down >= end).astype(jnp.int32)
        tile_across = tile_across + (across >= end).astype(jnp.int32)
    out[...] = jnp.where(tile_down == tile_across, 0.0, MASKED_SCORE)


def tile_bias(sizes, rows):
    return pl.pallas_call(
        tile_bias_kernel,
        out_shape=jax.ShapeDtypeStruct((rows, rows), jnp.float32),
        in_specs=[SMEM],
        out_specs=VMEM,
        name="tile_bias",
        compiler_params=pltpu.CompilerParams(vmem_limit_bytes=4 << 20),
        cost_estimate=pl.CostEstimate(flops=rows * rows, bytes_accessed=4 * rows * rows, transcendentals=0),
    )(sizes)


def temporal_kernel(keys_at, queries, bias_ref, *refs):
    outs, pieces = refs[len(refs) - queries :], refs[: len(refs) - queries]
    query_refs, group_refs = pieces[:queries], pieces[queries:]
    bias = bias_ref[...]
    keys = [ref[:, at : at + HD] for ref, at in zip(group_refs, keys_at)]
    values = [ref[:, at + HD : at + 2 * HD] for ref, at in zip(group_refs, keys_at)]
    for query_ref, out in zip(query_refs, outs):
        rows = query_ref[:, :HD]
        out[...] = attend([scores_of(rows, group) + bias for group in keys], values)


def temporal(bias, queries, groups, keys_at):
    rows = bias.shape[0]
    work = len(queries) * len(groups) * rows * rows
    return pl.pallas_call(
        lambda *refs: temporal_kernel(keys_at, len(queries), *refs),
        out_shape=[jax.ShapeDtypeStruct((rows, HD), queries[0].dtype)] * len(queries),
        in_specs=[VMEM] * (1 + len(queries) + len(groups)),
        out_specs=[VMEM] * len(queries),
        name="temporal",
        compiler_params=pltpu.CompilerParams(vmem_limit_bytes=16 << 20),
        cost_estimate=pl.CostEstimate(
            flops=4 * work * HD, bytes_accessed=4 * (len(queries) + len(groups)) * rows * HD, transcendentals=work
        ),
    )(bias, *queries, *groups)


def merge_kernel(heads_here, where_ref, ids_ref, given, *rest):
    pieces, out, sems = rest[:-2], rest[-2], rest[-1]
    copies = []
    for mask, piece in enumerate(pieces):
        head = head_of(ids_ref, where_ref[0] ^ mask, heads_here)
        copies.append(pltpu.make_async_copy(piece, out.at[:, columns(head)], sems.at[mask]))
        copies[-1].start()
    for copy in copies:
        copy.wait()


def merge(where, ids, out, pieces):
    rows, width = out.shape
    return pl.pallas_call(
        lambda *refs: merge_kernel(width // HD, *refs),
        out_shape=jax.ShapeDtypeStruct(out.shape, out.dtype),
        in_specs=[SMEM, SMEM, ANY] + [VMEM] * len(pieces),
        out_specs=ANY,
        scratch_shapes=[pltpu.SemaphoreType.DMA((len(pieces),))],
        input_output_aliases={2: 0},
        name="merge",
        compiler_params=pltpu.CompilerParams(vmem_limit_bytes=4 << 20),
        cost_estimate=pl.CostEstimate(flops=0, bytes_accessed=4 * len(pieces) * rows * HD, transcendentals=0),
    )(where, ids, out, *pieces)


def local_by_head(query, key_proj, value, block_mask, tile_sizes, temporal_ids):
    frames = lax.axis_size("frames")
    heads_here = block_mask.shape[0]
    where = jnp.stack([lax.axis_index("frames"), lax.axis_index("rep")]).astype(jnp.int32)

    def exchange(array, mask):
        return lax.ppermute(array, "frames", [(i, i ^ mask) for i in range(frames)])

    def swap(array):
        return lax.ppermute(array, "rep", [(0, 1), (1, 0)])

    *near, last = sorted(range(1, frames), key=lambda mask: (mask % 2 == 0, -mask))
    parts = [(m, "qkv") for m in near[:1]] + [(last, "kv")] + [(m, "qkv") for m in near[1:]] + [(last, "q"), (0, "qkv")]
    packed = pack(temporal_ids, query, key_proj, value, parts, heads_here)
    *travelling, own = packed
    arrived = [exchange(piece, mask) for piece, (mask, _) in zip(travelling, parts)]
    keys_sent, values_sent, *_ = lax.optimization_barrier((key_proj, value, *packed))
    key_other, value_other = swap(keys_sent), swap(values_sent)
    bias = tile_bias(tile_sizes, query.shape[0])
    out = spatial(where, temporal_ids, block_mask, query, key_proj, key_other, value, value_other)
    *arrived, late_query = arrived
    out, *arrived = lax.optimization_barrier((out, *arrived))
    groups = [own] + arrived
    keys_at = [HD] + [HD if names == "qkv" else 0 for _, names in parts[: len(arrived)]]
    whole = {mask: piece for piece, (mask, names) in zip(arrived, parts) if names == "qkv"}
    returned = {}
    (first,) = temporal(bias, [whole.pop(near[0])], groups, keys_at)
    returned[near[0]] = exchange(first, near[0])
    late_query, _ = lax.optimization_barrier((late_query, first))
    (second,) = temporal(bias, [late_query], groups, keys_at)
    returned[last] = exchange(second, last)
    own_query, *others, _ = lax.optimization_barrier((own, *whole.values(), second))
    mine, *rest = temporal(bias, [own_query, *others], groups, keys_at)
    for mask, piece in zip(whole, rest):
        returned[mask] = exchange(piece, mask)
    return merge(where, temporal_ids, out, [mine] + [returned[mask] for mask in range(1, frames)])


def local(query, key_proj, value, block_mask, tile_sizes, temporal_ids):
    frames, reps = lax.axis_size("frames"), lax.axis_size("rep")
    by_head = temporal_ids.shape[0] == frames and frames & (frames - 1) == 0 and reps == 2
    form = local_by_head if by_head else local_by_tile
    return form(query, key_proj, value, block_mask, tile_sizes, temporal_ids)


def solution(mesh):
    in_specs = (
        P(("groups", "frames", "rep"), "heads"),
        P(("groups", "frames", "rep"), "heads"),
        P(("groups", "frames", "rep"), "heads"),
        P("heads", None, None),
        P("rep", None),
        P("heads"),
    )
    out_specs = P(("groups", "frames", "rep"), "heads")
    return jax.shard_map(local, mesh=mesh, in_specs=in_specs, out_specs=out_specs, check_vma=False)
```

```python
import math

import jax
import jax.numpy as jnp
from jax import lax
from jax.experimental import pallas as pl
from jax.experimental.pallas import tpu as pltpu
from jax.sharding import PartitionSpec as P


HD = 128
BLK = 64


MASKED_SCORE = -1e30


def softmax_weights(scores):
    highest = jnp.max(scores, axis=-1, keepdims=True)
    raised = jnp.exp(scores - highest)
    return (raised / jnp.sum(raised, axis=-1, keepdims=True)).astype(jnp.bfloat16)


def select_heads(token_rows, picker):
    head_grid = token_rows.reshape(token_rows.shape[0], -1, HD)
    chosen = jnp.einsum(
        "rhd,th->rtd", head_grid, picker.astype(jnp.bfloat16), preferred_element_type=jnp.float32
    )
    return chosen.astype(jnp.bfloat16)


def spread_heads(head_grid, picker):
    return jnp.einsum(
        "rtd,th->rhd", head_grid, picker.astype(jnp.bfloat16), preferred_element_type=jnp.float32
    )


def local_by_tile(query, key_proj, value, block_mask, tile_sizes, temporal_ids):
    half_rows = query.shape[0]
    heads_here = block_mask.shape[0]
    temp_here = temporal_ids.shape[0]
    spat_here = heads_here - temp_here
    frame_blocks = block_mask.shape[1]
    frame_count = lax.axis_size("frames")
    slot_count = 2 * half_rows // frame_count
    score_scale = HD ** (-0.5)
    local_ids = temporal_ids - lax.axis_index("heads") * heads_here
    head_range = jnp.arange(heads_here, dtype=jnp.int32)
    pick_temp = local_ids[:, None] == head_range[None, :]
    temp_flag = jnp.sum(pick_temp.astype(jnp.int32), axis=0)
    spat_rank = jnp.cumsum(1 - temp_flag) - 1
    pick_spat = (spat_rank[None, :] == jnp.arange(spat_here, dtype=jnp.int32)[:, None]) & (
        temp_flag[None, :] == 0
    )
    tile_len = tile_sizes[0]
    starts = jnp.cumsum(tile_len) - tile_len
    slot_index = jnp.arange(slot_count, dtype=jnp.int32)
    source_rows = jnp.minimum(starts[:, None] + slot_index[None, :], half_rows - 1)
    frame_range = jnp.arange(frame_count, dtype=jnp.int32)
    own_len = jnp.sum(jnp.where(frame_range == lax.axis_index("frames"), tile_len, 0))
    key_live = jnp.tile(slot_index < own_len, frame_count)
    send_query = select_heads(query, pick_temp)[source_rows]
    send_keys = select_heads(key_proj, pick_temp)[source_rows]
    send_values = select_heads(value, pick_temp)[source_rows]
    tile_query = lax.all_to_all(send_query, "frames", split_axis=0, concat_axis=0, tiled=True)
    tile_keys = lax.all_to_all(send_keys, "frames", split_axis=0, concat_axis=0, tiled=True)
    tile_values = lax.all_to_all(send_values, "frames", split_axis=0, concat_axis=0, tiled=True)
    item_count = tile_query.shape[2]
    flat_query = tile_query.reshape(frame_count * slot_count, item_count, HD)
    flat_keys = tile_keys.reshape(frame_count * slot_count, item_count, HD)
    flat_values = tile_values.reshape(frame_count * slot_count, item_count, HD)
    scores = (
        jnp.einsum("qhd,khd->hqk", flat_query, flat_keys, preferred_element_type=jnp.float32)
        * score_scale
    )
    scores = jnp.where(key_live[None, None, :], scores, MASKED_SCORE)
    weights = softmax_weights(scores)
    tile_out = jnp.einsum(
        "hqk,khd->qhd", weights, flat_values, preferred_element_type=jnp.float32
    ).astype(jnp.bfloat16)
    returned = lax.all_to_all(
        tile_out.reshape(frame_count, slot_count, item_count, HD),
        "frames",
        split_axis=0,
        concat_axis=0,
        tiled=True,
    )
    own_keys = select_heads(key_proj, pick_spat)
    own_values = select_heads(value, pick_spat)
    spat_keys, spat_values = (
        lax.all_gather(own_keys, "rep", axis=0, tiled=True),
        lax.all_gather(own_values, "rep", axis=0, tiled=True),
    )
    spat_query = select_heads(query, pick_spat)
    spat_mask = (
        jnp.einsum("hij,th->tij", block_mask.astype(jnp.float32), pick_spat.astype(jnp.float32))
        > 0.5
    )
    query_blocks = half_rows // BLK
    mask_rows = lax.dynamic_slice_in_dim(
        spat_mask, lax.axis_index("rep") * query_blocks, query_blocks, 1
    )
    scores = (
        jnp.einsum("qhd,khd->hqk", spat_query, spat_keys, preferred_element_type=jnp.float32)
        * score_scale
    )
    shaped = scores.reshape(spat_here, query_blocks, BLK, frame_blocks, BLK)
    shaped = jnp.where(mask_rows[:, :, None, :, None], shaped, MASKED_SCORE)
    weights = softmax_weights(shaped.reshape(spat_here, half_rows, frame_blocks * BLK))
    spat_out = jnp.einsum(
        "hqk,khd->qhd", weights, spat_values, preferred_element_type=jnp.float32
    ).astype(jnp.bfloat16)
    positions = jnp.arange(half_rows, dtype=jnp.int32)
    tile_ends = starts + tile_len
    tile_of = jnp.sum((positions[:, None] >= tile_ends[None, :]).astype(jnp.int32), axis=1)
    picked_start = jnp.sum(
        jnp.where(tile_of[:, None] == frame_range[None, :], starts[None, :], 0), axis=1
    )
    flat_index = tile_of * slot_count + positions - picked_start
    temp_out = returned.reshape(frame_count * slot_count, temp_here, HD)[flat_index]
    combined = spread_heads(spat_out, pick_spat) + spread_heads(temp_out, pick_temp)
    return combined.astype(jnp.bfloat16).reshape(half_rows, heads_here * HD)


EXP2_SCALE = HD ** -0.5 * math.log2(math.e)
HBM = pl.BlockSpec(memory_space=pltpu.HBM)
ANY = pl.BlockSpec(memory_space=pl.ANY)
SMEM = pl.BlockSpec(memory_space=pltpu.SMEM)
VMEM = pl.BlockSpec(memory_space=pltpu.VMEM)


def scores_of(rows, keys):
    return lax.dot_general(rows, keys, (((1,), (1,)), ((), ())), preferred_element_type=jnp.float32)


def attend(scores, values):
    highest = scores[0].max(axis=-1, keepdims=True)
    for more in scores[1:]:
        highest = jnp.maximum(highest, more.max(axis=-1, keepdims=True))
    total, out = 0.0, 0.0
    for group, group_values in zip(scores, values):
        raised = jnp.exp2((group - highest) * EXP2_SCALE)
        total = total + raised.sum(axis=-1, keepdims=True)
        out = out + jnp.dot(raised.astype(jnp.bfloat16), group_values, preferred_element_type=jnp.float32)
    return (out / total).astype(jnp.bfloat16)


def columns(index):
    return pl.ds(pl.multiple_of(index * HD, HD), HD)


def head_of(ids_ref, slot, heads_here):
    return lax.rem(ids_ref[slot], heads_here)


def pack_kernel(heads_here, parts, ids_hbm, query, key_proj, value, *rest):
    outs, ids_ref, sems = rest[: len(parts)], rest[-2], rest[-1]
    sources = {"q": query, "k": key_proj, "v": value}
    fetch = pltpu.make_async_copy(ids_hbm, ids_ref, sems.at[0])
    fetch.start()
    frame = lax.axis_index("frames")
    fetch.wait()
    copies = []
    for out, (mask, names) in zip(outs, parts):
        head = head_of(ids_ref, frame ^ mask, heads_here)
        for place, name in enumerate(names):
            copies.append(
                pltpu.make_async_copy(
                    sources[name].at[:, columns(head)],
                    out.at[:, place * HD : (place + 1) * HD],
                    sems.at[len(copies) + 1],
                )
            )
            copies[-1].start()
    for copy in copies:
        copy.wait()


def pack(ids, query, key_proj, value, parts, heads_here):
    rows = query.shape[0]
    count = sum(len(names) for _, names in parts)
    return pl.pallas_call(
        lambda *refs: pack_kernel(heads_here, parts, *refs),
        out_shape=[pltpu.VMEM((rows, len(names) * HD), query.dtype) for _, names in parts],
        in_specs=[HBM] * 4,
        out_specs=[VMEM] * len(parts),
        scratch_shapes=[pltpu.SMEM(ids.shape, jnp.int32), pltpu.SemaphoreType.DMA((count + 1,))],
        name="pack",
        compiler_params=pltpu.CompilerParams(vmem_limit_bytes=4 << 20),
        cost_estimate=pl.CostEstimate(flops=0, bytes_accessed=4 * count * rows * HD, transcendentals=0),
    )(*(pltpu.with_memory_space_constraint(array, pltpu.HBM) for array in (ids, query, key_proj, value)))


def spatial_kernel(first, heads_ref, mask_ref, query, key_own, key_other, value_own, value_other, *rest):
    out = rest[-1]
    rows = query.shape[0]
    own_blocks, frame_blocks = rows // BLK, mask_ref.shape[-1]
    rep = lax.axis_index("rep")
    block = lax.broadcasted_iota(jnp.int32, (frame_blocks, 2 * rows), 1) // BLK
    block = lax.rem(block + rep * own_blocks, frame_blocks)
    spread = (block == lax.broadcasted_iota(jnp.int32, block.shape, 0)).astype(jnp.float32)
    mask = mask_ref[heads_ref[first + pl.program_id(0)]].astype(jnp.float32)
    seen = jnp.dot(mask, spread, preferred_element_type=jnp.float32)
    seen = jnp.where(rep == 0, seen[:own_blocks], seen[own_blocks:])
    bias = jnp.where(seen > 0.5, 0.0, MASKED_SCORE)
    bias = jnp.broadcast_to(bias[:, None, :], (own_blocks, BLK, 2 * rows)).reshape(rows, 2 * rows)
    own = scores_of(query[...], key_own[...]) + bias[:, :rows]
    other = scores_of(query[...], key_other[...]) + bias[:, rows:]
    out[...] = attend([own, other], [value_own[...], value_other[...]])


def spatial(heads, first, count, mask, query, key_own, key_other, value_own, value_other, out=None):
    rows, width = query.shape
    piece = pl.BlockSpec((rows, HD), lambda i, heads_ref: (0, heads_ref[first + i]))
    whole_mask = pl.BlockSpec(mask.shape, lambda i, heads_ref: (0, 0, 0))
    given = () if out is None else (out,)
    query, key_own, value_own = (pltpu.with_memory_space_constraint(x, pltpu.HBM) for x in (query, key_own, value_own))
    return pl.pallas_call(
        lambda *refs: spatial_kernel(first, *refs),
        out_shape=jax.ShapeDtypeStruct((rows, width), query.dtype),
        grid_spec=pltpu.PrefetchScalarGridSpec(
            num_scalar_prefetch=1,
            grid=(count,),
            in_specs=[whole_mask] + [piece] * 5 + [ANY] * len(given),
            out_specs=piece,
        ),
        input_output_aliases={7: 0} if given else {},
        name="spatial",
        compiler_params=pltpu.CompilerParams(vmem_limit_bytes=16 << 20),
        cost_estimate=pl.CostEstimate(
            flops=8 * rows * rows * HD * count, bytes_accessed=12 * rows * HD * count, transcendentals=2 * rows * rows * count
        ),
    )(heads, mask, query, key_own, key_other, value_own, value_other, *given)


def spatial_heads(ids, heads_here):
    head = jnp.arange(heads_here, dtype=jnp.int32)
    kept = jnp.all(lax.rem(ids, heads_here)[None, :] != head[:, None], axis=1)
    rank = jnp.sum((head[None, :] < head[:, None]) & kept[None, :], axis=1)
    place = jnp.arange(heads_here - ids.shape[0], dtype=jnp.int32)
    return jnp.sum(jnp.where(kept[None, :] & (rank[None, :] == place[:, None]), head[None, :], 0), axis=1)


def tile_bias_kernel(sizes_ref, out):
    rows = out.shape[0]
    down = lax.broadcasted_iota(jnp.int32, (rows, 1), 0)
    across = lax.broadcasted_iota(jnp.int32, (1, rows), 1)
    tile_down, tile_across, end = jnp.zeros_like(down), jnp.zeros_like(across), 0
    for tile in range(sizes_ref.shape[1]):
        end = end + sizes_ref[0, tile]
        tile_down = tile_down + (down >= end).astype(jnp.int32)
        tile_across = tile_across + (across >= end).astype(jnp.int32)
    out[...] = jnp.where(tile_down == tile_across, 0.0, MASKED_SCORE)


def tile_bias(sizes, rows):
    return pl.pallas_call(
        tile_bias_kernel,
        out_shape=jax.ShapeDtypeStruct((rows, rows), jnp.float32),
        in_specs=[SMEM],
        out_specs=VMEM,
        name="tile_bias",
        compiler_params=pltpu.CompilerParams(vmem_limit_bytes=4 << 20),
        cost_estimate=pl.CostEstimate(flops=rows * rows, bytes_accessed=4 * rows * rows, transcendentals=0),
    )(sizes)


def temporal_kernel(keys_at, queries, bias_ref, *refs):
    outs, pieces = refs[len(refs) - queries :], refs[: len(refs) - queries]
    query_refs, group_refs = pieces[:queries], pieces[queries:]
    bias = bias_ref[...]
    keys = [ref[:, at : at + HD] for ref, at in zip(group_refs, keys_at)]
    values = [ref[:, at + HD : at + 2 * HD] for ref, at in zip(group_refs, keys_at)]
    for query_ref, out in zip(query_refs, outs):
        rows = query_ref[:, :HD]
        out[...] = attend([scores_of(rows, group) + bias for group in keys], values)


def temporal(bias, queries, groups, keys_at):
    rows = bias.shape[0]
    work = len(queries) * len(groups) * rows * rows
    return pl.pallas_call(
        lambda *refs: temporal_kernel(keys_at, len(queries), *refs),
        out_shape=[jax.ShapeDtypeStruct((rows, HD), queries[0].dtype)] * len(queries),
        in_specs=[VMEM] * (1 + len(queries) + len(groups)),
        out_specs=[VMEM] * len(queries),
        name="temporal",
        compiler_params=pltpu.CompilerParams(vmem_limit_bytes=16 << 20),
        cost_estimate=pl.CostEstimate(
            flops=4 * work * HD, bytes_accessed=4 * (len(queries) + len(groups)) * rows * HD, transcendentals=work
        ),
    )(bias, *queries, *groups)


def merge_kernel(heads_here, ids_ref, given, *rest):
    pieces, out, sems = rest[:-2], rest[-2], rest[-1]
    frame = lax.axis_index("frames")
    copies = []
    for mask, piece in enumerate(pieces):
        head = head_of(ids_ref, frame ^ mask, heads_here)
        copies.append(pltpu.make_async_copy(piece, out.at[:, columns(head)], sems.at[mask]))
        copies[-1].start()
    for copy in copies:
        copy.wait()


def merge(ids, out, pieces):
    rows, width = out.shape
    return pl.pallas_call(
        lambda *refs: merge_kernel(width // HD, *refs),
        out_shape=jax.ShapeDtypeStruct(out.shape, out.dtype),
        in_specs=[SMEM, ANY] + [VMEM] * len(pieces),
        out_specs=ANY,
        scratch_shapes=[pltpu.SemaphoreType.DMA((len(pieces),))],
        input_output_aliases={1: 0},
        name="merge",
        compiler_params=pltpu.CompilerParams(vmem_limit_bytes=4 << 20),
        cost_estimate=pl.CostEstimate(flops=0, bytes_accessed=4 * len(pieces) * rows * HD, transcendentals=0),
    )(ids, out, *pieces)


def local_by_head(query, key_proj, value, block_mask, tile_sizes, temporal_ids):
    frames = lax.axis_size("frames")
    heads_here = block_mask.shape[0]

    def exchange(array, mask):
        return lax.ppermute(array, "frames", [(i, i ^ mask) for i in range(frames)])

    def swap(array):
        return lax.ppermute(array, "rep", [(0, 1), (1, 0)])

    *near, last = sorted(range(1, frames), key=lambda mask: (mask % 2 == 0, -mask))
    parts = [(m, "qkv") for m in near[:1]] + [(last, "kv")] + [(m, "qkv") for m in near[1:]] + [(last, "q"), (0, "qkv")]
    packed = pack(temporal_ids, query, key_proj, value, parts, heads_here)
    *travelling, own = packed
    arrived = [exchange(piece, mask) for piece, (mask, _) in zip(travelling, parts)]
    keys_sent, values_sent, *_ = lax.optimization_barrier((key_proj, value, *packed))
    key_other, value_other = swap(keys_sent), swap(values_sent)
    bias = tile_bias(tile_sizes, query.shape[0])
    heads = spatial_heads(temporal_ids, heads_here)
    inputs = (block_mask, query, key_proj, key_other, value, value_other)
    early = heads.shape[0] * 5 // 8
    out = spatial(heads, 0, early, *inputs)
    *arrived, late_query = arrived
    out, *arrived = lax.optimization_barrier((out, *arrived))
    groups = [own] + arrived
    keys_at = [HD] + [HD if names == "qkv" else 0 for _, names in parts[: len(arrived)]]
    turns = [(mask, piece) for piece, (mask, names) in zip(arrived, parts) if names == "qkv"]
    turns = turns + [(last, late_query), (0, own)]
    returned = {}
    for mask, rows in turns:
        (done,) = temporal(bias, [rows], groups, keys_at)
        returned[mask] = exchange(done, mask) if mask else done
    out = spatial(heads, early, heads.shape[0] - early, *inputs, out)
    return merge(temporal_ids, out, [returned[mask] for mask in range(frames)])


def local(query, key_proj, value, block_mask, tile_sizes, temporal_ids):
    frames, reps = lax.axis_size("frames"), lax.axis_size("rep")
    by_head = temporal_ids.shape[0] == frames and frames & (frames - 1) == 0 and reps == 2
    form = local_by_head if by_head else local_by_tile
    return form(query, key_proj, value, block_mask, tile_sizes, temporal_ids)


def solution(mesh):
    in_specs = (
        P(("groups", "frames", "rep"), "heads"),
        P(("groups", "frames", "rep"), "heads"),
        P(("groups", "frames", "rep"), "heads"),
        P("heads", None, None),
        P("rep", None),
        P("heads"),
    )
    out_specs = P(("groups", "frames", "rep"), "heads")
    return jax.shard_map(local, mesh=mesh, in_specs=in_specs, out_specs=out_specs, check_vma=False)
```

```python
import math

import jax
import jax.numpy as jnp
from jax import lax
from jax.experimental import pallas as pl
from jax.experimental.pallas import tpu as pltpu
from jax.sharding import PartitionSpec as P


HD = 128
BLK = 64


MASKED_SCORE = -1e30


def softmax_weights(scores):
    highest = jnp.max(scores, axis=-1, keepdims=True)
    raised = jnp.exp(scores - highest)
    return (raised / jnp.sum(raised, axis=-1, keepdims=True)).astype(jnp.bfloat16)


def select_heads(token_rows, picker):
    head_grid = token_rows.reshape(token_rows.shape[0], -1, HD)
    chosen = jnp.einsum(
        "rhd,th->rtd", head_grid, picker.astype(jnp.bfloat16), preferred_element_type=jnp.float32
    )
    return chosen.astype(jnp.bfloat16)


def spread_heads(head_grid, picker):
    return jnp.einsum(
        "rtd,th->rhd", head_grid, picker.astype(jnp.bfloat16), preferred_element_type=jnp.float32
    )


def local_by_tile(query, key_proj, value, block_mask, tile_sizes, temporal_ids):
    half_rows = query.shape[0]
    heads_here = block_mask.shape[0]
    temp_here = temporal_ids.shape[0]
    spat_here = heads_here - temp_here
    frame_blocks = block_mask.shape[1]
    frame_count = lax.axis_size("frames")
    slot_count = 2 * half_rows // frame_count
    score_scale = HD ** (-0.5)
    local_ids = temporal_ids - lax.axis_index("heads") * heads_here
    head_range = jnp.arange(heads_here, dtype=jnp.int32)
    pick_temp = local_ids[:, None] == head_range[None, :]
    temp_flag = jnp.sum(pick_temp.astype(jnp.int32), axis=0)
    spat_rank = jnp.cumsum(1 - temp_flag) - 1
    pick_spat = (spat_rank[None, :] == jnp.arange(spat_here, dtype=jnp.int32)[:, None]) & (
        temp_flag[None, :] == 0
    )
    tile_len = tile_sizes[0]
    starts = jnp.cumsum(tile_len) - tile_len
    slot_index = jnp.arange(slot_count, dtype=jnp.int32)
    source_rows = jnp.minimum(starts[:, None] + slot_index[None, :], half_rows - 1)
    frame_range = jnp.arange(frame_count, dtype=jnp.int32)
    own_len = jnp.sum(jnp.where(frame_range == lax.axis_index("frames"), tile_len, 0))
    key_live = jnp.tile(slot_index < own_len, frame_count)
    send_query = select_heads(query, pick_temp)[source_rows]
    send_keys = select_heads(key_proj, pick_temp)[source_rows]
    send_values = select_heads(value, pick_temp)[source_rows]
    tile_query = lax.all_to_all(send_query, "frames", split_axis=0, concat_axis=0, tiled=True)
    tile_keys = lax.all_to_all(send_keys, "frames", split_axis=0, concat_axis=0, tiled=True)
    tile_values = lax.all_to_all(send_values, "frames", split_axis=0, concat_axis=0, tiled=True)
    item_count = tile_query.shape[2]
    flat_query = tile_query.reshape(frame_count * slot_count, item_count, HD)
    flat_keys = tile_keys.reshape(frame_count * slot_count, item_count, HD)
    flat_values = tile_values.reshape(frame_count * slot_count, item_count, HD)
    scores = (
        jnp.einsum("qhd,khd->hqk", flat_query, flat_keys, preferred_element_type=jnp.float32)
        * score_scale
    )
    scores = jnp.where(key_live[None, None, :], scores, MASKED_SCORE)
    weights = softmax_weights(scores)
    tile_out = jnp.einsum(
        "hqk,khd->qhd", weights, flat_values, preferred_element_type=jnp.float32
    ).astype(jnp.bfloat16)
    returned = lax.all_to_all(
        tile_out.reshape(frame_count, slot_count, item_count, HD),
        "frames",
        split_axis=0,
        concat_axis=0,
        tiled=True,
    )
    own_keys = select_heads(key_proj, pick_spat)
    own_values = select_heads(value, pick_spat)
    spat_keys, spat_values = (
        lax.all_gather(own_keys, "rep", axis=0, tiled=True),
        lax.all_gather(own_values, "rep", axis=0, tiled=True),
    )
    spat_query = select_heads(query, pick_spat)
    spat_mask = (
        jnp.einsum("hij,th->tij", block_mask.astype(jnp.float32), pick_spat.astype(jnp.float32))
        > 0.5
    )
    query_blocks = half_rows // BLK
    mask_rows = lax.dynamic_slice_in_dim(
        spat_mask, lax.axis_index("rep") * query_blocks, query_blocks, 1
    )
    scores = (
        jnp.einsum("qhd,khd->hqk", spat_query, spat_keys, preferred_element_type=jnp.float32)
        * score_scale
    )
    shaped = scores.reshape(spat_here, query_blocks, BLK, frame_blocks, BLK)
    shaped = jnp.where(mask_rows[:, :, None, :, None], shaped, MASKED_SCORE)
    weights = softmax_weights(shaped.reshape(spat_here, half_rows, frame_blocks * BLK))
    spat_out = jnp.einsum(
        "hqk,khd->qhd", weights, spat_values, preferred_element_type=jnp.float32
    ).astype(jnp.bfloat16)
    positions = jnp.arange(half_rows, dtype=jnp.int32)
    tile_ends = starts + tile_len
    tile_of = jnp.sum((positions[:, None] >= tile_ends[None, :]).astype(jnp.int32), axis=1)
    picked_start = jnp.sum(
        jnp.where(tile_of[:, None] == frame_range[None, :], starts[None, :], 0), axis=1
    )
    flat_index = tile_of * slot_count + positions - picked_start
    temp_out = returned.reshape(frame_count * slot_count, temp_here, HD)[flat_index]
    combined = spread_heads(spat_out, pick_spat) + spread_heads(temp_out, pick_temp)
    return combined.astype(jnp.bfloat16).reshape(half_rows, heads_here * HD)


EXP2_SCALE = HD ** -0.5 * math.log2(math.e)
HBM = pl.BlockSpec(memory_space=pltpu.HBM)
ANY = pl.BlockSpec(memory_space=pl.ANY)
SMEM = pl.BlockSpec(memory_space=pltpu.SMEM)
VMEM = pl.BlockSpec(memory_space=pltpu.VMEM)


def scores_of(rows, keys):
    return lax.dot_general(rows, keys, (((1,), (1,)), ((), ())), preferred_element_type=jnp.float32)


def attend(scores, values):
    highest = scores[0]
    for more in scores[1:]:
        highest = jnp.maximum(highest, more)
    highest = highest.max(axis=-1, keepdims=True)
    raised = [jnp.exp2((group - highest) * EXP2_SCALE) for group in scores]
    total = raised[0]
    for more in raised[1:]:
        total = total + more
    out = jnp.dot(raised[0].astype(jnp.bfloat16), values[0], preferred_element_type=jnp.float32)
    for weights, group_values in zip(raised[1:], values[1:]):
        out = out + jnp.dot(weights.astype(jnp.bfloat16), group_values, preferred_element_type=jnp.float32)
    return (out / total.sum(axis=-1, keepdims=True)).astype(jnp.bfloat16)


def columns(index):
    return pl.ds(pl.multiple_of(index * HD, HD), HD)


def head_of(ids_ref, slot, heads_here):
    return lax.rem(ids_ref[slot], heads_here)


def pack_kernel(heads_here, parts, ids_hbm, query, key_proj, value, *rest):
    outs, ids_ref, sems = rest[: len(parts)], rest[-2], rest[-1]
    sources = {"q": query, "k": key_proj, "v": value}
    fetch = pltpu.make_async_copy(ids_hbm, ids_ref, sems.at[0])
    fetch.start()
    frame = lax.axis_index("frames")
    fetch.wait()
    copies = []
    for out, (mask, names) in zip(outs, parts):
        head = head_of(ids_ref, frame ^ mask, heads_here)
        for place, name in enumerate(names):
            copies.append(
                pltpu.make_async_copy(
                    sources[name].at[:, columns(head)],
                    out.at[:, place * HD : (place + 1) * HD],
                    sems.at[len(copies) + 1],
                )
            )
            copies[-1].start()
    for copy in copies:
        copy.wait()


def pack(ids, query, key_proj, value, parts, heads_here):
    rows = query.shape[0]
    count = sum(len(names) for _, names in parts)
    return pl.pallas_call(
        lambda *refs: pack_kernel(heads_here, parts, *refs),
        out_shape=[pltpu.VMEM((rows, len(names) * HD), query.dtype) for _, names in parts],
        in_specs=[HBM] * 4,
        out_specs=[VMEM] * len(parts),
        scratch_shapes=[pltpu.SMEM(ids.shape, jnp.int32), pltpu.SemaphoreType.DMA((count + 1,))],
        name="pack",
        compiler_params=pltpu.CompilerParams(vmem_limit_bytes=4 << 20),
        cost_estimate=pl.CostEstimate(flops=0, bytes_accessed=4 * count * rows * HD, transcendentals=0),
    )(*(pltpu.with_memory_space_constraint(array, pltpu.HBM) for array in (ids, query, key_proj, value)))


def spatial_kernel(heads_ref, mask_ref, query, key_own, key_other, value_own, value_other, out, seen_ref, fetched, stage, arrive, leave):
    rows, count = query.shape[0], heads_ref.shape[0]
    own_blocks, frame_blocks = rows // BLK, mask_ref.shape[-1]
    coming, going = [], []
    for item in range(count):
        coming.append(
            [
                pltpu.make_async_copy(
                    source.at[:, columns(heads_ref[item])], fetched.at[item, :, i * HD : (i + 1) * HD], arrive.at[item, i]
                )
                for i, source in enumerate((query, key_own, value_own))
            ]
        )
        for copy in coming[-1]:
            copy.start()
    rep = lax.axis_index("rep")
    block = lax.broadcasted_iota(jnp.int32, (frame_blocks, 2 * rows), 1) // BLK
    block = lax.rem(block + rep * own_blocks, frame_blocks)
    spread = (block == lax.broadcasted_iota(jnp.int32, block.shape, 0)).astype(jnp.float32)
    seen_ref[...] = jnp.dot(mask_ref[...].astype(jnp.float32), spread, preferred_element_type=jnp.float32)
    for copies in coming:
        for copy in copies:
            copy.wait()
    for item in range(count):
        head = heads_ref[item]
        seen = seen_ref[pl.ds(pl.multiple_of(head * frame_blocks, frame_blocks), frame_blocks), :]
        seen = jnp.where(rep == 0, seen[:own_blocks], seen[own_blocks:])
        bias = jnp.where(seen > 0.5, 0.0, MASKED_SCORE)
        bias = jnp.broadcast_to(bias[:, None, :], (own_blocks, BLK, 2 * rows)).reshape(rows, 2 * rows)
        asked = fetched[item, :, :HD]
        own = scores_of(asked, fetched[item, :, HD : 2 * HD]) + bias[:, :rows]
        other = scores_of(asked, key_other[:, columns(head)]) + bias[:, rows:]
        stage[item] = attend([own, other], [fetched[item, :, 2 * HD :], value_other[:, columns(head)]])
        if (item + 1) % 4 == 0 or item + 1 == count:
            for sent in range(len(going), item + 1):
                going.append(pltpu.make_async_copy(stage.at[sent], out.at[:, columns(heads_ref[sent])], leave.at[sent]))
                going[-1].start()
    for copy in going:
        copy.wait()


def spatial(heads, mask, query, key_own, key_other, value_own, value_other):
    rows, width = query.shape
    count, blocks = heads.shape[0], mask.shape[-1]
    query, key_own, value_own = (pltpu.with_memory_space_constraint(x, pltpu.HBM) for x in (query, key_own, value_own))
    return pl.pallas_call(
        spatial_kernel,
        out_shape=jax.ShapeDtypeStruct((rows, width), query.dtype),
        in_specs=[SMEM, VMEM, HBM, HBM, VMEM, HBM, VMEM],
        out_specs=HBM,
        scratch_shapes=[
            pltpu.VMEM((mask.shape[0] * blocks, 2 * rows), jnp.float32),
            pltpu.VMEM((count, rows, 3 * HD), query.dtype),
            pltpu.VMEM((count, rows, HD), query.dtype),
            pltpu.SemaphoreType.DMA((count, 3)),
            pltpu.SemaphoreType.DMA((count,)),
        ],
        name="spatial",
        compiler_params=pltpu.CompilerParams(vmem_limit_bytes=16 << 20),
        cost_estimate=pl.CostEstimate(
            flops=8 * rows * rows * HD * count, bytes_accessed=12 * rows * HD * count, transcendentals=2 * rows * rows * count
        ),
    )(heads, mask.reshape(-1, blocks), query, key_own, key_other, value_own, value_other)


def spatial_heads(ids, heads_here):
    head = jnp.arange(heads_here, dtype=jnp.int32)
    kept = jnp.all(lax.rem(ids, heads_here)[None, :] != head[:, None], axis=1)
    rank = jnp.sum((head[None, :] < head[:, None]) & kept[None, :], axis=1)
    place = jnp.arange(heads_here - ids.shape[0], dtype=jnp.int32)
    return jnp.sum(jnp.where(kept[None, :] & (rank[None, :] == place[:, None]), head[None, :], 0), axis=1)


def tile_bias_kernel(sizes_ref, out):
    rows = out.shape[0]
    down = lax.broadcasted_iota(jnp.int32, (rows, 1), 0)
    across = lax.broadcasted_iota(jnp.int32, (1, rows), 1)
    tile_down, tile_across, end = jnp.zeros_like(down), jnp.zeros_like(across), 0
    for tile in range(sizes_ref.shape[1]):
        end = end + sizes_ref[0, tile]
        tile_down = tile_down + (down >= end).astype(jnp.int32)
        tile_across = tile_across + (across >= end).astype(jnp.int32)
    out[...] = jnp.where(tile_down == tile_across, 0.0, MASKED_SCORE)


def tile_bias(sizes, rows):
    return pl.pallas_call(
        tile_bias_kernel,
        out_shape=jax.ShapeDtypeStruct((rows, rows), jnp.float32),
        in_specs=[SMEM],
        out_specs=VMEM,
        name="tile_bias",
        compiler_params=pltpu.CompilerParams(vmem_limit_bytes=4 << 20),
        cost_estimate=pl.CostEstimate(flops=rows * rows, bytes_accessed=4 * rows * rows, transcendentals=0),
    )(sizes)


def temporal_kernel(keys_at, queries, bias_ref, *refs):
    outs, pieces = refs[len(refs) - queries :], refs[: len(refs) - queries]
    query_refs, group_refs = pieces[:queries], pieces[queries:]
    bias = bias_ref[...]
    keys = [ref[:, at : at + HD] for ref, at in zip(group_refs, keys_at)]
    values = [ref[:, at + HD : at + 2 * HD] for ref, at in zip(group_refs, keys_at)]
    for query_ref, out in zip(query_refs, outs):
        rows = query_ref[:, :HD]
        out[...] = attend([scores_of(rows, group) + bias for group in keys], values)


def temporal(bias, queries, groups, keys_at):
    rows = bias.shape[0]
    work = len(queries) * len(groups) * rows * rows
    return pl.pallas_call(
        lambda *refs: temporal_kernel(keys_at, len(queries), *refs),
        out_shape=[jax.ShapeDtypeStruct((rows, HD), queries[0].dtype)] * len(queries),
        in_specs=[VMEM] * (1 + len(queries) + len(groups)),
        out_specs=[VMEM] * len(queries),
        name="temporal",
        compiler_params=pltpu.CompilerParams(vmem_limit_bytes=16 << 20),
        cost_estimate=pl.CostEstimate(
            flops=4 * work * HD, bytes_accessed=4 * (len(queries) + len(groups)) * rows * HD, transcendentals=work
        ),
    )(bias, *queries, *groups)


def merge_kernel(heads_here, ids_ref, given, *rest):
    pieces, out, sems = rest[:-2], rest[-2], rest[-1]
    frame = lax.axis_index("frames")
    copies = []
    for mask, piece in enumerate(pieces):
        head = head_of(ids_ref, frame ^ mask, heads_here)
        copies.append(pltpu.make_async_copy(piece, out.at[:, columns(head)], sems.at[mask]))
        copies[-1].start()
    for copy in copies:
        copy.wait()


def merge(ids, out, pieces):
    rows, width = out.shape
    return pl.pallas_call(
        lambda *refs: merge_kernel(width // HD, *refs),
        out_shape=jax.ShapeDtypeStruct(out.shape, out.dtype),
        in_specs=[SMEM, ANY] + [VMEM] * len(pieces),
        out_specs=ANY,
        scratch_shapes=[pltpu.SemaphoreType.DMA((len(pieces),))],
        input_output_aliases={1: 0},
        name="merge",
        compiler_params=pltpu.CompilerParams(vmem_limit_bytes=4 << 20),
        cost_estimate=pl.CostEstimate(flops=0, bytes_accessed=4 * len(pieces) * rows * HD, transcendentals=0),
    )(ids, out, *pieces)


def local_by_head(query, key_proj, value, block_mask, tile_sizes, temporal_ids):
    frames = lax.axis_size("frames")
    heads_here = block_mask.shape[0]

    def exchange(array, mask):
        return lax.ppermute(array, "frames", [(i, i ^ mask) for i in range(frames)])

    def swap(array):
        return lax.ppermute(array, "rep", [(0, 1), (1, 0)])

    first, last = frames - 1, frames // 2
    near = [m for m in range(1, first) if m != last]
    parts = [(first, "qkv"), (last, "kv")] + [(m, "qkv") for m in near] + [(last, "q"), (0, "qkv")]
    packed = pack(temporal_ids, query, key_proj, value, parts, heads_here)
    *travelling, own = packed
    arrived = [exchange(piece, mask) for piece, (mask, _) in zip(travelling, parts)]
    keys_sent, values_sent, *_ = lax.optimization_barrier((key_proj, value, *packed))
    key_other, value_other = swap(keys_sent), swap(values_sent)
    bias = tile_bias(tile_sizes, query.shape[0])
    heads = spatial_heads(temporal_ids, heads_here)
    bias, *inputs = lax.optimization_barrier((bias, key_other, value_other))
    out = spatial(heads, block_mask, query, key_proj, inputs[0], value, inputs[1])
    *arrived, late_query = arrived
    out, *arrived = lax.optimization_barrier((out, *arrived))
    groups = [own] + arrived
    keys_at = [HD] + [HD if names == "qkv" else 0 for _, names in parts[: len(arrived)]]
    turns = [(mask, piece) for piece, (mask, names) in zip(arrived, parts) if names == "qkv"]
    turns = turns[:1] + [(last, late_query)] + turns[1:] + [(0, own)]
    order = turns[:1] + turns[2:-1] + turns[1:2] + turns[-1:]
    attended = {}
    for mask, rows in order:
        (attended[mask],) = temporal(bias, [rows], groups, keys_at)
    returned = {0: attended[0]}
    for mask, _ in turns[:-1]:
        returned[mask] = exchange(attended[mask], mask)
    return merge(temporal_ids, out, [returned[mask] for mask in range(frames)])


def local(query, key_proj, value, block_mask, tile_sizes, temporal_ids):
    frames, reps = lax.axis_size("frames"), lax.axis_size("rep")
    by_head = temporal_ids.shape[0] == frames and frames & (frames - 1) == 0 and reps == 2
    form = local_by_head if by_head else local_by_tile
    return form(query, key_proj, value, block_mask, tile_sizes, temporal_ids)


def solution(mesh):
    in_specs = (
        P(("groups", "frames", "rep"), "heads"),
        P(("groups", "frames", "rep"), "heads"),
        P(("groups", "frames", "rep"), "heads"),
        P("heads", None, None),
        P("rep", None),
        P("heads"),
    )
    out_specs = P(("groups", "frames", "rep"), "heads")
    return jax.shard_map(local, mesh=mesh, in_specs=in_specs, out_specs=out_specs, check_vma=False)
```

```python
import math

import jax
import jax.numpy as jnp
from jax import lax
from jax.experimental import pallas as pl
from jax.experimental.pallas import tpu as pltpu
from jax.sharding import PartitionSpec as P


HD = 128
BLK = 64


MASKED_SCORE = -1e30


def softmax_weights(scores):
    highest = jnp.max(scores, axis=-1, keepdims=True)
    raised = jnp.exp(scores - highest)
    return (raised / jnp.sum(raised, axis=-1, keepdims=True)).astype(jnp.bfloat16)


def select_heads(token_rows, picker):
    head_grid = token_rows.reshape(token_rows.shape[0], -1, HD)
    chosen = jnp.einsum(
        "rhd,th->rtd", head_grid, picker.astype(jnp.bfloat16), preferred_element_type=jnp.float32
    )
    return chosen.astype(jnp.bfloat16)


def spread_heads(head_grid, picker):
    return jnp.einsum(
        "rtd,th->rhd", head_grid, picker.astype(jnp.bfloat16), preferred_element_type=jnp.float32
    )


def local_by_tile(query, key_proj, value, block_mask, tile_sizes, temporal_ids):
    half_rows = query.shape[0]
    heads_here = block_mask.shape[0]
    temp_here = temporal_ids.shape[0]
    spat_here = heads_here - temp_here
    frame_blocks = block_mask.shape[1]
    frame_count = lax.axis_size("frames")
    slot_count = 2 * half_rows // frame_count
    score_scale = HD ** (-0.5)
    local_ids = temporal_ids - lax.axis_index("heads") * heads_here
    head_range = jnp.arange(heads_here, dtype=jnp.int32)
    pick_temp = local_ids[:, None] == head_range[None, :]
    temp_flag = jnp.sum(pick_temp.astype(jnp.int32), axis=0)
    spat_rank = jnp.cumsum(1 - temp_flag) - 1
    pick_spat = (spat_rank[None, :] == jnp.arange(spat_here, dtype=jnp.int32)[:, None]) & (
        temp_flag[None, :] == 0
    )
    tile_len = tile_sizes[0]
    starts = jnp.cumsum(tile_len) - tile_len
    slot_index = jnp.arange(slot_count, dtype=jnp.int32)
    source_rows = jnp.minimum(starts[:, None] + slot_index[None, :], half_rows - 1)
    frame_range = jnp.arange(frame_count, dtype=jnp.int32)
    own_len = jnp.sum(jnp.where(frame_range == lax.axis_index("frames"), tile_len, 0))
    key_live = jnp.tile(slot_index < own_len, frame_count)
    send_query = select_heads(query, pick_temp)[source_rows]
    send_keys = select_heads(key_proj, pick_temp)[source_rows]
    send_values = select_heads(value, pick_temp)[source_rows]
    tile_query = lax.all_to_all(send_query, "frames", split_axis=0, concat_axis=0, tiled=True)
    tile_keys = lax.all_to_all(send_keys, "frames", split_axis=0, concat_axis=0, tiled=True)
    tile_values = lax.all_to_all(send_values, "frames", split_axis=0, concat_axis=0, tiled=True)
    item_count = tile_query.shape[2]
    flat_query = tile_query.reshape(frame_count * slot_count, item_count, HD)
    flat_keys = tile_keys.reshape(frame_count * slot_count, item_count, HD)
    flat_values = tile_values.reshape(frame_count * slot_count, item_count, HD)
    scores = (
        jnp.einsum("qhd,khd->hqk", flat_query, flat_keys, preferred_element_type=jnp.float32)
        * score_scale
    )
    scores = jnp.where(key_live[None, None, :], scores, MASKED_SCORE)
    weights = softmax_weights(scores)
    tile_out = jnp.einsum(
        "hqk,khd->qhd", weights, flat_values, preferred_element_type=jnp.float32
    ).astype(jnp.bfloat16)
    returned = lax.all_to_all(
        tile_out.reshape(frame_count, slot_count, item_count, HD),
        "frames",
        split_axis=0,
        concat_axis=0,
        tiled=True,
    )
    own_keys = select_heads(key_proj, pick_spat)
    own_values = select_heads(value, pick_spat)
    spat_keys, spat_values = (
        lax.all_gather(own_keys, "rep", axis=0, tiled=True),
        lax.all_gather(own_values, "rep", axis=0, tiled=True),
    )
    spat_query = select_heads(query, pick_spat)
    spat_mask = (
        jnp.einsum("hij,th->tij", block_mask.astype(jnp.float32), pick_spat.astype(jnp.float32))
        > 0.5
    )
    query_blocks = half_rows // BLK
    mask_rows = lax.dynamic_slice_in_dim(
        spat_mask, lax.axis_index("rep") * query_blocks, query_blocks, 1
    )
    scores = (
        jnp.einsum("qhd,khd->hqk", spat_query, spat_keys, preferred_element_type=jnp.float32)
        * score_scale
    )
    shaped = scores.reshape(spat_here, query_blocks, BLK, frame_blocks, BLK)
    shaped = jnp.where(mask_rows[:, :, None, :, None], shaped, MASKED_SCORE)
    weights = softmax_weights(shaped.reshape(spat_here, half_rows, frame_blocks * BLK))
    spat_out = jnp.einsum(
        "hqk,khd->qhd", weights, spat_values, preferred_element_type=jnp.float32
    ).astype(jnp.bfloat16)
    positions = jnp.arange(half_rows, dtype=jnp.int32)
    tile_ends = starts + tile_len
    tile_of = jnp.sum((positions[:, None] >= tile_ends[None, :]).astype(jnp.int32), axis=1)
    picked_start = jnp.sum(
        jnp.where(tile_of[:, None] == frame_range[None, :], starts[None, :], 0), axis=1
    )
    flat_index = tile_of * slot_count + positions - picked_start
    temp_out = returned.reshape(frame_count * slot_count, temp_here, HD)[flat_index]
    combined = spread_heads(spat_out, pick_spat) + spread_heads(temp_out, pick_temp)
    return combined.astype(jnp.bfloat16).reshape(half_rows, heads_here * HD)


EXP2_SCALE = HD ** -0.5 * math.log2(math.e)
HBM = pl.BlockSpec(memory_space=pltpu.HBM)
ANY = pl.BlockSpec(memory_space=pl.ANY)
SMEM = pl.BlockSpec(memory_space=pltpu.SMEM)
VMEM = pl.BlockSpec(memory_space=pltpu.VMEM)


def scores_of(rows, keys):
    return lax.dot_general(rows, keys, (((1,), (1,)), ((), ())), preferred_element_type=jnp.float32)


def attend(scores, values):
    highest = scores[0]
    for more in scores[1:]:
        highest = jnp.maximum(highest, more)
    highest = highest.max(axis=-1, keepdims=True)
    raised = [jnp.exp2((group - highest) * EXP2_SCALE) for group in scores]
    total = raised[0]
    for more in raised[1:]:
        total = total + more
    out = jnp.dot(raised[0].astype(jnp.bfloat16), values[0], preferred_element_type=jnp.float32)
    for weights, group_values in zip(raised[1:], values[1:]):
        out = out + jnp.dot(weights.astype(jnp.bfloat16), group_values, preferred_element_type=jnp.float32)
    return (out / total.sum(axis=-1, keepdims=True)).astype(jnp.bfloat16)


def columns(index):
    return pl.ds(pl.multiple_of(index * HD, HD), HD)


def head_of(ids_ref, slot, heads_here):
    return lax.rem(ids_ref[slot], heads_here)


def pack_kernel(heads_here, parts, ids_hbm, query, key_proj, value, *rest):
    outs, ids_ref, sems = rest[: len(parts)], rest[-2], rest[-1]
    sources = {"q": query, "k": key_proj, "v": value}
    fetch = pltpu.make_async_copy(ids_hbm, ids_ref, sems.at[0])
    fetch.start()
    frame = lax.axis_index("frames")
    fetch.wait()
    copies = []
    for out, (mask, names) in zip(outs, parts):
        head = head_of(ids_ref, frame ^ mask, heads_here)
        for place, name in enumerate(names):
            copies.append(
                pltpu.make_async_copy(
                    sources[name].at[:, columns(head)],
                    out.at[:, place * HD : (place + 1) * HD],
                    sems.at[len(copies) + 1],
                )
            )
            copies[-1].start()
    for copy in copies:
        copy.wait()


def pack(ids, query, key_proj, value, parts, heads_here):
    rows = query.shape[0]
    count = sum(len(names) for _, names in parts)
    return pl.pallas_call(
        lambda *refs: pack_kernel(heads_here, parts, *refs),
        out_shape=[pltpu.VMEM((rows, len(names) * HD), query.dtype) for _, names in parts],
        in_specs=[HBM] * 4,
        out_specs=[VMEM] * len(parts),
        scratch_shapes=[pltpu.SMEM(ids.shape, jnp.int32), pltpu.SemaphoreType.DMA((count + 1,))],
        name="pack",
        compiler_params=pltpu.CompilerParams(vmem_limit_bytes=4 << 20),
        cost_estimate=pl.CostEstimate(flops=0, bytes_accessed=4 * count * rows * HD, transcendentals=0),
    )(*(pltpu.with_memory_space_constraint(array, pltpu.HBM) for array in (ids, query, key_proj, value)))


def spatial_kernel(heads_ref, mask_ref, query, key_own, key_other, value_own, value_other, out, bias_ref, asked, held, stage, arrive, leave):
    rows, count = query.shape[0], heads_ref.shape[0]
    own_blocks, frame_blocks = rows // BLK, mask_ref.shape[-1]
    coming = []
    for item in range(count):
        here = columns(heads_ref[item])
        for source, target in (
            (query, asked.at[item]),
            (key_own, held.at[item, 0, 0]),
            (value_own, held.at[item, 1, 0]),
            (key_other, held.at[item, 0, 1]),
            (value_other, held.at[item, 1, 1]),
        ):
            coming.append(pltpu.make_async_copy(source.at[:, here], target, arrive.at[len(coming)]))
            coming[-1].start()
    rep = lax.axis_index("rep")
    block = lax.broadcasted_iota(jnp.int32, (frame_blocks, 2 * rows), 1) // BLK
    block = lax.rem(block + rep * own_blocks, frame_blocks)
    spread = (block == lax.broadcasted_iota(jnp.int32, block.shape, 0)).astype(jnp.float32)
    for item in range(count):
        mask = mask_ref[heads_ref[item]].astype(jnp.float32)
        mask = jnp.where(rep == 0, mask[:own_blocks], mask[own_blocks:])
        seen = jnp.dot(mask, spread, preferred_element_type=jnp.float32)
        bias_ref[item] = jnp.where(seen > 0.5, 0.0, MASKED_SCORE)
    for copy in coming:
        copy.wait()
    going = []
    for item in range(count):
        bias = jnp.broadcast_to(bias_ref[item][:, None, :], (own_blocks, BLK, 2 * rows)).reshape(rows, 2 * rows)
        scores = [scores_of(asked[item], held[item, 0, half]) + bias[:, half * rows : (half + 1) * rows] for half in range(2)]
        stage[item] = attend(scores, [held[item, 1, half] for half in range(2)])
        if (item + 1) % 4 == 0 or item + 1 == count:
            for sent in range(len(going), item + 1):
                going.append(pltpu.make_async_copy(stage.at[sent], out.at[:, columns(heads_ref[sent])], leave.at[sent]))
                going[-1].start()
    for copy in going:
        copy.wait()


def spatial(heads, mask, query, key_own, key_other, value_own, value_other):
    rows, width = query.shape
    count = heads.shape[0]
    query, key_own, value_own = (pltpu.with_memory_space_constraint(x, pltpu.HBM) for x in (query, key_own, value_own))
    return pl.pallas_call(
        spatial_kernel,
        out_shape=jax.ShapeDtypeStruct((rows, width), query.dtype),
        in_specs=[SMEM, VMEM, HBM, HBM, VMEM, HBM, VMEM],
        out_specs=HBM,
        scratch_shapes=[
            pltpu.VMEM((count, rows // BLK, 2 * rows), jnp.float32),
            pltpu.VMEM((count, rows, HD), query.dtype),
            pltpu.VMEM((count, 2, 2, rows, HD), query.dtype),
            pltpu.VMEM((count, rows, HD), query.dtype),
            pltpu.SemaphoreType.DMA((5 * count,)),
            pltpu.SemaphoreType.DMA((count,)),
        ],
        name="spatial",
        compiler_params=pltpu.CompilerParams(vmem_limit_bytes=16 << 20),
        cost_estimate=pl.CostEstimate(
            flops=8 * rows * rows * HD * count, bytes_accessed=12 * rows * HD * count, transcendentals=2 * rows * rows * count
        ),
    )(heads, mask, query, key_own, key_other, value_own, value_other)


def spatial_heads(ids, heads_here):
    head = jnp.arange(heads_here, dtype=jnp.int32)
    kept = jnp.all(lax.rem(ids, heads_here)[None, :] != head[:, None], axis=1)
    rank = jnp.sum((head[None, :] < head[:, None]) & kept[None, :], axis=1)
    place = jnp.arange(heads_here - ids.shape[0], dtype=jnp.int32)
    return jnp.sum(jnp.where(kept[None, :] & (rank[None, :] == place[:, None]), head[None, :], 0), axis=1)


def tile_bias_kernel(sizes_ref, out):
    rows = out.shape[0]
    down = lax.broadcasted_iota(jnp.int32, (rows, 1), 0)
    across = lax.broadcasted_iota(jnp.int32, (1, rows), 1)
    tile_down, tile_across, end = jnp.zeros_like(down), jnp.zeros_like(across), 0
    for tile in range(sizes_ref.shape[1]):
        end = end + sizes_ref[0, tile]
        tile_down = tile_down + (down >= end).astype(jnp.int32)
        tile_across = tile_across + (across >= end).astype(jnp.int32)
    out[...] = jnp.where(tile_down == tile_across, 0.0, MASKED_SCORE)


def tile_bias(sizes, rows):
    return pl.pallas_call(
        tile_bias_kernel,
        out_shape=jax.ShapeDtypeStruct((rows, rows), jnp.float32),
        in_specs=[SMEM],
        out_specs=VMEM,
        name="tile_bias",
        compiler_params=pltpu.CompilerParams(vmem_limit_bytes=4 << 20),
        cost_estimate=pl.CostEstimate(flops=rows * rows, bytes_accessed=4 * rows * rows, transcendentals=0),
    )(sizes)


def temporal_kernel(keys_at, queries, bias_ref, *refs):
    outs, pieces = refs[len(refs) - queries :], refs[: len(refs) - queries]
    query_refs, group_refs = pieces[:queries], pieces[queries:]
    bias = bias_ref[...]
    keys = [ref[:, at : at + HD] for ref, at in zip(group_refs, keys_at)]
    values = [ref[:, at + HD : at + 2 * HD] for ref, at in zip(group_refs, keys_at)]
    for query_ref, out in zip(query_refs, outs):
        rows = query_ref[:, :HD]
        out[...] = attend([scores_of(rows, group) + bias for group in keys], values)


def temporal(bias, queries, groups, keys_at):
    rows = bias.shape[0]
    work = len(queries) * len(groups) * rows * rows
    return pl.pallas_call(
        lambda *refs: temporal_kernel(keys_at, len(queries), *refs),
        out_shape=[jax.ShapeDtypeStruct((rows, HD), queries[0].dtype)] * len(queries),
        in_specs=[VMEM] * (1 + len(queries) + len(groups)),
        out_specs=[VMEM] * len(queries),
        name="temporal",
        compiler_params=pltpu.CompilerParams(vmem_limit_bytes=16 << 20),
        cost_estimate=pl.CostEstimate(
            flops=4 * work * HD, bytes_accessed=4 * (len(queries) + len(groups)) * rows * HD, transcendentals=work
        ),
    )(bias, *queries, *groups)


def merge_kernel(heads_here, ids_ref, given, *rest):
    pieces, out, sems = rest[:-2], rest[-2], rest[-1]
    frame = lax.axis_index("frames")
    ids = lax.rem(ids_ref[...], heads_here).astype(jnp.float32)
    slot = lax.broadcasted_iota(jnp.int32, ids.shape, 1)
    copies = []
    for mask, piece in enumerate(pieces):
        head = jnp.sum(jnp.where(slot == frame ^ mask, ids, 0.0)).astype(jnp.int32)
        copies.append(pltpu.make_async_copy(piece, out.at[:, columns(head)], sems.at[mask]))
        copies[-1].start()
    for copy in copies:
        copy.wait()


def merge(ids, out, pieces):
    rows, width = out.shape
    return pl.pallas_call(
        lambda *refs: merge_kernel(width // HD, *refs),
        out_shape=jax.ShapeDtypeStruct(out.shape, out.dtype),
        in_specs=[VMEM, ANY] + [VMEM] * len(pieces),
        out_specs=ANY,
        scratch_shapes=[pltpu.SemaphoreType.DMA((len(pieces),))],
        input_output_aliases={1: 0},
        name="merge",
        compiler_params=pltpu.CompilerParams(vmem_limit_bytes=4 << 20),
        cost_estimate=pl.CostEstimate(flops=0, bytes_accessed=4 * len(pieces) * rows * HD, transcendentals=0),
    )(ids.reshape(1, -1), out, *pieces)


PLAN = ("s3", "k2", "s1", "wk", "wv", "x", "q2", "a31", "b3", "b1", "a2", "b2", "a0")
NAMES = {"s": "qkv", "k": "kv", "q": "q"}


def local_by_head(query, key_proj, value, block_mask, tile_sizes, temporal_ids):
    frames = lax.axis_size("frames")
    heads_here = block_mask.shape[0]

    def exchange(array, mask):
        return lax.ppermute(array, "frames", [(i, i ^ mask) for i in range(frames)])

    sends = [step for step in PLAN if step[0] in NAMES]
    parts = [(int(step[1:]), NAMES[step[0]]) for step in sends] + [(0, "qkv")]
    packed = dict(zip(sends + ["own"], pack(temporal_ids, query, key_proj, value, parts, heads_here)))
    keys_sent, values_sent, *_ = lax.optimization_barrier((key_proj, value, *packed.values()))
    swapped = {"wk": keys_sent, "wv": values_sent}
    bias = tile_bias(tile_sizes, query.shape[0])
    heads = spatial_heads(temporal_ids, heads_here)
    queries, groups, keys_at, attended, returned = {0: packed["own"]}, [packed["own"]], [HD], {}, {}
    for step in PLAN:
        kind, masks = step[0], [int(digit) for digit in step[1:] if digit.isdigit()]
        if kind in NAMES:
            arrived = exchange(packed[step], masks[0])
            if kind in "sq":
                queries[masks[0]] = arrived
            if kind in "sk":
                groups.append(arrived)
                keys_at.append(HD if kind == "s" else 0)
        elif kind == "w":
            swapped[step] = lax.ppermute(swapped[step], "rep", [(0, 1), (1, 0)])
        elif kind == "x":
            bias, *others = lax.optimization_barrier((bias, swapped["wk"], swapped["wv"]))
            out = spatial(heads, block_mask, query, key_proj, others[0], value, others[1])
        elif kind == "a":
            attended.update(zip(masks, temporal(bias, [queries[mask] for mask in masks], groups, keys_at)))
        elif kind == "b":
            returned[masks[0]] = exchange(attended[masks[0]], masks[0])
    returned[0] = attended[0]
    return merge(temporal_ids, out, [returned[mask] for mask in range(frames)])


def local(query, key_proj, value, block_mask, tile_sizes, temporal_ids):
    frames, reps = lax.axis_size("frames"), lax.axis_size("rep")
    by_head = temporal_ids.shape[0] == frames == 4 and reps == 2
    form = local_by_head if by_head else local_by_tile
    return form(query, key_proj, value, block_mask, tile_sizes, temporal_ids)


def solution(mesh):
    in_specs = (
        P(("groups", "frames", "rep"), "heads"),
        P(("groups", "frames", "rep"), "heads"),
        P(("groups", "frames", "rep"), "heads"),
        P("heads", None, None),
        P("rep", None),
        P("heads"),
    )
    out_specs = P(("groups", "frames", "rep"), "heads")
    return jax.shard_map(local, mesh=mesh, in_specs=in_specs, out_specs=out_specs, check_vma=False)
```

```python
import math

import jax
import jax.numpy as jnp
from jax import lax
from jax.experimental import pallas as pl
from jax.experimental.pallas import tpu as pltpu
from jax.sharding import PartitionSpec as P


HD = 128
BLK = 64


MASKED_SCORE = -1e30


def softmax_weights(scores):
    highest = jnp.max(scores, axis=-1, keepdims=True)
    raised = jnp.exp(scores - highest)
    return (raised / jnp.sum(raised, axis=-1, keepdims=True)).astype(jnp.bfloat16)


def select_heads(token_rows, picker):
    head_grid = token_rows.reshape(token_rows.shape[0], -1, HD)
    chosen = jnp.einsum(
        "rhd,th->rtd", head_grid, picker.astype(jnp.bfloat16), preferred_element_type=jnp.float32
    )
    return chosen.astype(jnp.bfloat16)


def spread_heads(head_grid, picker):
    return jnp.einsum(
        "rtd,th->rhd", head_grid, picker.astype(jnp.bfloat16), preferred_element_type=jnp.float32
    )


def local_by_tile(query, key_proj, value, block_mask, tile_sizes, temporal_ids):
    half_rows = query.shape[0]
    heads_here = block_mask.shape[0]
    temp_here = temporal_ids.shape[0]
    spat_here = heads_here - temp_here
    frame_blocks = block_mask.shape[1]
    frame_count = lax.axis_size("frames")
    slot_count = 2 * half_rows // frame_count
    score_scale = HD ** (-0.5)
    local_ids = temporal_ids - lax.axis_index("heads") * heads_here
    head_range = jnp.arange(heads_here, dtype=jnp.int32)
    pick_temp = local_ids[:, None] == head_range[None, :]
    temp_flag = jnp.sum(pick_temp.astype(jnp.int32), axis=0)
    spat_rank = jnp.cumsum(1 - temp_flag) - 1
    pick_spat = (spat_rank[None, :] == jnp.arange(spat_here, dtype=jnp.int32)[:, None]) & (
        temp_flag[None, :] == 0
    )
    tile_len = tile_sizes[0]
    starts = jnp.cumsum(tile_len) - tile_len
    slot_index = jnp.arange(slot_count, dtype=jnp.int32)
    source_rows = jnp.minimum(starts[:, None] + slot_index[None, :], half_rows - 1)
    frame_range = jnp.arange(frame_count, dtype=jnp.int32)
    own_len = jnp.sum(jnp.where(frame_range == lax.axis_index("frames"), tile_len, 0))
    key_live = jnp.tile(slot_index < own_len, frame_count)
    send_query = select_heads(query, pick_temp)[source_rows]
    send_keys = select_heads(key_proj, pick_temp)[source_rows]
    send_values = select_heads(value, pick_temp)[source_rows]
    tile_query = lax.all_to_all(send_query, "frames", split_axis=0, concat_axis=0, tiled=True)
    tile_keys = lax.all_to_all(send_keys, "frames", split_axis=0, concat_axis=0, tiled=True)
    tile_values = lax.all_to_all(send_values, "frames", split_axis=0, concat_axis=0, tiled=True)
    item_count = tile_query.shape[2]
    flat_query = tile_query.reshape(frame_count * slot_count, item_count, HD)
    flat_keys = tile_keys.reshape(frame_count * slot_count, item_count, HD)
    flat_values = tile_values.reshape(frame_count * slot_count, item_count, HD)
    scores = (
        jnp.einsum("qhd,khd->hqk", flat_query, flat_keys, preferred_element_type=jnp.float32)
        * score_scale
    )
    scores = jnp.where(key_live[None, None, :], scores, MASKED_SCORE)
    weights = softmax_weights(scores)
    tile_out = jnp.einsum(
        "hqk,khd->qhd", weights, flat_values, preferred_element_type=jnp.float32
    ).astype(jnp.bfloat16)
    returned = lax.all_to_all(
        tile_out.reshape(frame_count, slot_count, item_count, HD),
        "frames",
        split_axis=0,
        concat_axis=0,
        tiled=True,
    )
    own_keys = select_heads(key_proj, pick_spat)
    own_values = select_heads(value, pick_spat)
    spat_keys, spat_values = (
        lax.all_gather(own_keys, "rep", axis=0, tiled=True),
        lax.all_gather(own_values, "rep", axis=0, tiled=True),
    )
    spat_query = select_heads(query, pick_spat)
    spat_mask = (
        jnp.einsum("hij,th->tij", block_mask.astype(jnp.float32), pick_spat.astype(jnp.float32))
        > 0.5
    )
    query_blocks = half_rows // BLK
    mask_rows = lax.dynamic_slice_in_dim(
        spat_mask, lax.axis_index("rep") * query_blocks, query_blocks, 1
    )
    scores = (
        jnp.einsum("qhd,khd->hqk", spat_query, spat_keys, preferred_element_type=jnp.float32)
        * score_scale
    )
    shaped = scores.reshape(spat_here, query_blocks, BLK, frame_blocks, BLK)
    shaped = jnp.where(mask_rows[:, :, None, :, None], shaped, MASKED_SCORE)
    weights = softmax_weights(shaped.reshape(spat_here, half_rows, frame_blocks * BLK))
    spat_out = jnp.einsum(
        "hqk,khd->qhd", weights, spat_values, preferred_element_type=jnp.float32
    ).astype(jnp.bfloat16)
    positions = jnp.arange(half_rows, dtype=jnp.int32)
    tile_ends = starts + tile_len
    tile_of = jnp.sum((positions[:, None] >= tile_ends[None, :]).astype(jnp.int32), axis=1)
    picked_start = jnp.sum(
        jnp.where(tile_of[:, None] == frame_range[None, :], starts[None, :], 0), axis=1
    )
    flat_index = tile_of * slot_count + positions - picked_start
    temp_out = returned.reshape(frame_count * slot_count, temp_here, HD)[flat_index]
    combined = spread_heads(spat_out, pick_spat) + spread_heads(temp_out, pick_temp)
    return combined.astype(jnp.bfloat16).reshape(half_rows, heads_here * HD)


EXP2_SCALE = HD ** -0.5 * math.log2(math.e)
HBM = pl.BlockSpec(memory_space=pltpu.HBM)
ANY = pl.BlockSpec(memory_space=pl.ANY)
SMEM = pl.BlockSpec(memory_space=pltpu.SMEM)
VMEM = pl.BlockSpec(memory_space=pltpu.VMEM)


def scores_of(rows, keys):
    return lax.dot_general(rows, keys, (((1,), (1,)), ((), ())), preferred_element_type=jnp.float32)


def attend(scores, values, ones=False):
    highest = scores[0]
    for more in scores[1:]:
        highest = jnp.maximum(highest, more)
    highest = highest.max(axis=-1, keepdims=True)
    out, total = 0.0, 0.0
    for group, group_values in zip(scores, values):
        raised = jnp.exp2((group - highest) * EXP2_SCALE)
        if ones:
            group_values = jnp.concatenate([group_values, jnp.ones_like(group_values)], axis=1)
        else:
            total = total + raised
        out = out + jnp.dot(raised.astype(jnp.bfloat16), group_values, preferred_element_type=jnp.float32)
    total = out[:, HD:] if ones else total.sum(axis=-1, keepdims=True)
    return (out[:, :HD] / total).astype(jnp.bfloat16)


def columns(index):
    return pl.ds(pl.multiple_of(index * HD, HD), HD)


def head_of(ids_ref, slot, heads_here):
    return lax.rem(ids_ref[slot], heads_here)


def pack_kernel(heads_here, parts, ids_hbm, query, key_proj, value, *rest):
    outs, ids_ref, sems = rest[: len(parts)], rest[-2], rest[-1]
    sources = {"q": query, "k": key_proj, "v": value}
    fetch = pltpu.make_async_copy(ids_hbm, ids_ref, sems.at[0])
    fetch.start()
    frame = lax.axis_index("frames")
    fetch.wait()
    copies = []
    for out, (mask, names) in zip(outs, parts):
        head = head_of(ids_ref, frame ^ mask, heads_here)
        for place, name in enumerate(names):
            copies.append(
                pltpu.make_async_copy(
                    sources[name].at[:, columns(head)],
                    out.at[:, place * HD : (place + 1) * HD],
                    sems.at[len(copies) + 1],
                )
            )
            copies[-1].start()
    for copy in copies:
        copy.wait()


def pack(ids, query, key_proj, value, parts, heads_here):
    rows = query.shape[0]
    count = sum(len(names) for _, names in parts)
    return pl.pallas_call(
        lambda *refs: pack_kernel(heads_here, parts, *refs),
        out_shape=[pltpu.VMEM((rows, len(names) * HD), query.dtype) for _, names in parts],
        in_specs=[HBM] * 4,
        out_specs=[VMEM] * len(parts),
        scratch_shapes=[pltpu.SMEM(ids.shape, jnp.int32), pltpu.SemaphoreType.DMA((count + 1,))],
        name="pack",
        compiler_params=pltpu.CompilerParams(vmem_limit_bytes=4 << 20),
        cost_estimate=pl.CostEstimate(flops=0, bytes_accessed=4 * count * rows * HD, transcendentals=0),
    )(*(pltpu.with_memory_space_constraint(array, pltpu.HBM) for array in (ids, query, key_proj, value)))


def spatial_kernel(heads_ref, mask_ref, query, key_own, key_other, value_own, value_other, out, bias_ref, asked, held, stage, arrive, leave):
    rows, count = query.shape[0], heads_ref.shape[0]
    own_blocks, frame_blocks = rows // BLK, mask_ref.shape[-1]
    coming = []
    for item in range(count):
        here = columns(heads_ref[item])
        for source, target in (
            (query, asked.at[item]),
            (key_own, held.at[item, 0, 0]),
            (value_own, held.at[item, 1, 0]),
            (key_other, held.at[item, 0, 1]),
            (value_other, held.at[item, 1, 1]),
        ):
            coming.append(pltpu.make_async_copy(source.at[:, here], target, arrive.at[len(coming)]))
            coming[-1].start()
    rep = lax.axis_index("rep")
    block = lax.broadcasted_iota(jnp.int32, (frame_blocks, 2 * rows), 1) // BLK
    block = lax.rem(block + rep * own_blocks, frame_blocks)
    spread = (block == lax.broadcasted_iota(jnp.int32, block.shape, 0)).astype(jnp.float32)
    for item in range(count):
        mask = mask_ref[heads_ref[item]].astype(jnp.float32)
        mask = jnp.where(rep == 0, mask[:own_blocks], mask[own_blocks:])
        seen = jnp.dot(mask, spread, preferred_element_type=jnp.float32)
        bias_ref[item] = jnp.where(seen > 0.5, 0.0, MASKED_SCORE)
    for copy in coming:
        copy.wait()
    going = []
    for item in range(count):
        bias = jnp.broadcast_to(bias_ref[item][:, None, :], (own_blocks, BLK, 2 * rows)).reshape(rows, 2 * rows)
        scores = [scores_of(asked[item], held[item, 0, half]) + bias[:, half * rows : (half + 1) * rows] for half in range(2)]
        stage[item] = attend(scores, [held[item, 1, half] for half in range(2)], ones=True)
        if (item + 1) % 4 == 0 or item + 1 == count:
            for sent in range(len(going), item + 1):
                going.append(pltpu.make_async_copy(stage.at[sent], out.at[:, columns(heads_ref[sent])], leave.at[sent]))
                going[-1].start()
    for copy in going:
        copy.wait()


def spatial(heads, mask, query, key_own, key_other, value_own, value_other):
    rows, width = query.shape
    count = heads.shape[0]
    query, key_own, value_own = (pltpu.with_memory_space_constraint(x, pltpu.HBM) for x in (query, key_own, value_own))
    return pl.pallas_call(
        spatial_kernel,
        out_shape=jax.ShapeDtypeStruct((rows, width), query.dtype),
        in_specs=[SMEM, VMEM, HBM, HBM, VMEM, HBM, VMEM],
        out_specs=HBM,
        scratch_shapes=[
            pltpu.VMEM((count, rows // BLK, 2 * rows), jnp.float32),
            pltpu.VMEM((count, rows, HD), query.dtype),
            pltpu.VMEM((count, 2, 2, rows, HD), query.dtype),
            pltpu.VMEM((count, rows, HD), query.dtype),
            pltpu.SemaphoreType.DMA((5 * count,)),
            pltpu.SemaphoreType.DMA((count,)),
        ],
        name="spatial",
        compiler_params=pltpu.CompilerParams(vmem_limit_bytes=16 << 20),
        cost_estimate=pl.CostEstimate(
            flops=8 * rows * rows * HD * count, bytes_accessed=12 * rows * HD * count, transcendentals=2 * rows * rows * count
        ),
    )(heads, mask, query, key_own, key_other, value_own, value_other)


def spatial_heads(ids, heads_here):
    head = jnp.arange(heads_here, dtype=jnp.int32)
    kept = jnp.all(lax.rem(ids, heads_here)[None, :] != head[:, None], axis=1)
    rank = jnp.sum((head[None, :] < head[:, None]) & kept[None, :], axis=1)
    place = jnp.arange(heads_here - ids.shape[0], dtype=jnp.int32)
    return jnp.sum(jnp.where(kept[None, :] & (rank[None, :] == place[:, None]), head[None, :], 0), axis=1)


def tile_bias_kernel(sizes_ref, out):
    rows = out.shape[0]
    down = lax.broadcasted_iota(jnp.int32, (rows, 1), 0)
    across = lax.broadcasted_iota(jnp.int32, (1, rows), 1)
    tile_down, tile_across, end = jnp.zeros_like(down), jnp.zeros_like(across), 0
    for tile in range(sizes_ref.shape[1]):
        end = end + sizes_ref[0, tile]
        tile_down = tile_down + (down >= end).astype(jnp.int32)
        tile_across = tile_across + (across >= end).astype(jnp.int32)
    out[...] = jnp.where(tile_down == tile_across, 0.0, MASKED_SCORE)


def tile_bias(sizes, rows):
    return pl.pallas_call(
        tile_bias_kernel,
        out_shape=jax.ShapeDtypeStruct((rows, rows), jnp.float32),
        in_specs=[SMEM],
        out_specs=VMEM,
        name="tile_bias",
        compiler_params=pltpu.CompilerParams(vmem_limit_bytes=4 << 20),
        cost_estimate=pl.CostEstimate(flops=rows * rows, bytes_accessed=4 * rows * rows, transcendentals=0),
    )(sizes)


def temporal_kernel(keys_at, queries, bias_ref, *refs):
    outs, pieces = refs[len(refs) - queries :], refs[: len(refs) - queries]
    query_refs, group_refs = pieces[:queries], pieces[queries:]
    bias = bias_ref[...]
    keys = [ref[:, at : at + HD] for ref, at in zip(group_refs, keys_at)]
    values = [ref[:, at + HD : at + 2 * HD] for ref, at in zip(group_refs, keys_at)]
    for query_ref, out in zip(query_refs, outs):
        rows = query_ref[:, :HD]
        out[...] = attend([scores_of(rows, group) + bias for group in keys], values)


def temporal(bias, queries, groups, keys_at):
    rows = bias.shape[0]
    work = len(queries) * len(groups) * rows * rows
    return pl.pallas_call(
        lambda *refs: temporal_kernel(keys_at, len(queries), *refs),
        out_shape=[jax.ShapeDtypeStruct((rows, HD), queries[0].dtype)] * len(queries),
        in_specs=[VMEM] * (1 + len(queries) + len(groups)),
        out_specs=[VMEM] * len(queries),
        name="temporal",
        compiler_params=pltpu.CompilerParams(vmem_limit_bytes=16 << 20),
        cost_estimate=pl.CostEstimate(
            flops=4 * work * HD, bytes_accessed=4 * (len(queries) + len(groups)) * rows * HD, transcendentals=work
        ),
    )(bias, *queries, *groups)


def merge_kernel(heads_here, ids_ref, given, *rest):
    pieces, out, sems = rest[:-2], rest[-2], rest[-1]
    frame = lax.axis_index("frames")
    ids = lax.rem(ids_ref[...], heads_here).astype(jnp.float32)
    slot = lax.broadcasted_iota(jnp.int32, ids.shape, 1)
    copies = []
    for mask, piece in enumerate(pieces):
        head = jnp.sum(jnp.where(slot == frame ^ mask, ids, 0.0)).astype(jnp.int32)
        copies.append(pltpu.make_async_copy(piece, out.at[:, columns(head)], sems.at[mask]))
        copies[-1].start()
    for copy in copies:
        copy.wait()


def merge(ids, out, pieces):
    rows, width = out.shape
    return pl.pallas_call(
        lambda *refs: merge_kernel(width // HD, *refs),
        out_shape=jax.ShapeDtypeStruct(out.shape, out.dtype),
        in_specs=[VMEM, ANY] + [VMEM] * len(pieces),
        out_specs=ANY,
        scratch_shapes=[pltpu.SemaphoreType.DMA((len(pieces),))],
        input_output_aliases={1: 0},
        name="merge",
        compiler_params=pltpu.CompilerParams(vmem_limit_bytes=4 << 20),
        cost_estimate=pl.CostEstimate(flops=0, bytes_accessed=4 * len(pieces) * rows * HD, transcendentals=0),
    )(ids.reshape(1, -1), out, *pieces)


PLAN = ("s3", "s1", "k2", "d", "wk", "wv", "x", "q2", "a31", "b3", "b1", "a2", "b2", "a0")
NAMES = {"s": "qkv", "k": "kv", "q": "q"}


def local_by_head(query, key_proj, value, block_mask, tile_sizes, temporal_ids):
    frames = lax.axis_size("frames")
    heads_here = block_mask.shape[0]

    def exchange(array, mask):
        return lax.ppermute(array, "frames", [(i, i ^ mask) for i in range(frames)])

    sends = [step for step in PLAN if step[0] in NAMES]
    parts = [(int(step[1:]), NAMES[step[0]]) for step in sends] + [(0, "qkv")]
    packed = dict(zip(sends + ["own"], pack(temporal_ids, query, key_proj, value, parts, heads_here)))
    keys_sent, values_sent, *_ = lax.optimization_barrier((key_proj, value, *packed.values()))
    swapped = {"wk": keys_sent, "wv": values_sent}
    heads = spatial_heads(temporal_ids, heads_here)
    queries, groups, keys_at, attended, returned = {0: packed["own"]}, [packed["own"]], [HD], {}, {}
    for step in PLAN:
        kind, masks = step[0], [int(digit) for digit in step[1:] if digit.isdigit()]
        if kind in NAMES:
            arrived = exchange(packed[step], masks[0])
            if kind in "sq":
                queries[masks[0]] = arrived
            if kind in "sk":
                groups.append(arrived)
                keys_at.append(HD if kind == "s" else 0)
        elif kind == "w":
            swapped[step] = lax.ppermute(swapped[step], "rep", [(0, 1), (1, 0)])
        elif kind == "x":
            out = spatial(heads, block_mask, query, key_proj, swapped["wk"], value, swapped["wv"])
        elif kind == "d":
            bias = tile_bias(tile_sizes, query.shape[0])
        elif kind == "a":
            attended.update(zip(masks, temporal(bias, [queries[mask] for mask in masks], groups, keys_at)))
        elif kind == "b":
            returned[masks[0]] = exchange(attended[masks[0]], masks[0])
    returned[0] = attended[0]
    return merge(temporal_ids, out, [returned[mask] for mask in range(frames)])


def local(query, key_proj, value, block_mask, tile_sizes, temporal_ids):
    frames, reps = lax.axis_size("frames"), lax.axis_size("rep")
    by_head = temporal_ids.shape[0] == frames == 4 and reps == 2
    form = local_by_head if by_head else local_by_tile
    return form(query, key_proj, value, block_mask, tile_sizes, temporal_ids)


def solution(mesh):
    in_specs = (
        P(("groups", "frames", "rep"), "heads"),
        P(("groups", "frames", "rep"), "heads"),
        P(("groups", "frames", "rep"), "heads"),
        P("heads", None, None),
        P("rep", None),
        P("heads"),
    )
    out_specs = P(("groups", "frames", "rep"), "heads")
    return jax.shard_map(local, mesh=mesh, in_specs=in_specs, out_specs=out_specs, check_vma=False)
```

```python
import math

import jax
import jax.numpy as jnp
from jax import lax
from jax.experimental import pallas as pl
from jax.experimental.pallas import tpu as pltpu
from jax.sharding import PartitionSpec as P


HD = 128
BLK = 64


MASKED_SCORE = -1e30


def softmax_weights(scores):
    highest = jnp.max(scores, axis=-1, keepdims=True)
    raised = jnp.exp(scores - highest)
    return (raised / jnp.sum(raised, axis=-1, keepdims=True)).astype(jnp.bfloat16)


def select_heads(token_rows, picker):
    head_grid = token_rows.reshape(token_rows.shape[0], -1, HD)
    chosen = jnp.einsum(
        "rhd,th->rtd", head_grid, picker.astype(jnp.bfloat16), preferred_element_type=jnp.float32
    )
    return chosen.astype(jnp.bfloat16)


def spread_heads(head_grid, picker):
    return jnp.einsum(
        "rtd,th->rhd", head_grid, picker.astype(jnp.bfloat16), preferred_element_type=jnp.float32
    )


def local_by_tile(query, key_proj, value, block_mask, tile_sizes, temporal_ids):
    half_rows = query.shape[0]
    heads_here = block_mask.shape[0]
    temp_here = temporal_ids.shape[0]
    spat_here = heads_here - temp_here
    frame_blocks = block_mask.shape[1]
    frame_count = lax.axis_size("frames")
    slot_count = 2 * half_rows // frame_count
    score_scale = HD ** (-0.5)
    local_ids = temporal_ids - lax.axis_index("heads") * heads_here
    head_range = jnp.arange(heads_here, dtype=jnp.int32)
    pick_temp = local_ids[:, None] == head_range[None, :]
    temp_flag = jnp.sum(pick_temp.astype(jnp.int32), axis=0)
    spat_rank = jnp.cumsum(1 - temp_flag) - 1
    pick_spat = (spat_rank[None, :] == jnp.arange(spat_here, dtype=jnp.int32)[:, None]) & (
        temp_flag[None, :] == 0
    )
    tile_len = tile_sizes[0]
    starts = jnp.cumsum(tile_len) - tile_len
    slot_index = jnp.arange(slot_count, dtype=jnp.int32)
    source_rows = jnp.minimum(starts[:, None] + slot_index[None, :], half_rows - 1)
    frame_range = jnp.arange(frame_count, dtype=jnp.int32)
    own_len = jnp.sum(jnp.where(frame_range == lax.axis_index("frames"), tile_len, 0))
    key_live = jnp.tile(slot_index < own_len, frame_count)
    send_query = select_heads(query, pick_temp)[source_rows]
    send_keys = select_heads(key_proj, pick_temp)[source_rows]
    send_values = select_heads(value, pick_temp)[source_rows]
    tile_query = lax.all_to_all(send_query, "frames", split_axis=0, concat_axis=0, tiled=True)
    tile_keys = lax.all_to_all(send_keys, "frames", split_axis=0, concat_axis=0, tiled=True)
    tile_values = lax.all_to_all(send_values, "frames", split_axis=0, concat_axis=0, tiled=True)
    item_count = tile_query.shape[2]
    flat_query = tile_query.reshape(frame_count * slot_count, item_count, HD)
    flat_keys = tile_keys.reshape(frame_count * slot_count, item_count, HD)
    flat_values = tile_values.reshape(frame_count * slot_count, item_count, HD)
    scores = (
        jnp.einsum("qhd,khd->hqk", flat_query, flat_keys, preferred_element_type=jnp.float32)
        * score_scale
    )
    scores = jnp.where(key_live[None, None, :], scores, MASKED_SCORE)
    weights = softmax_weights(scores)
    tile_out = jnp.einsum(
        "hqk,khd->qhd", weights, flat_values, preferred_element_type=jnp.float32
    ).astype(jnp.bfloat16)
    returned = lax.all_to_all(
        tile_out.reshape(frame_count, slot_count, item_count, HD),
        "frames",
        split_axis=0,
        concat_axis=0,
        tiled=True,
    )
    own_keys = select_heads(key_proj, pick_spat)
    own_values = select_heads(value, pick_spat)
    spat_keys, spat_values = (
        lax.all_gather(own_keys, "rep", axis=0, tiled=True),
        lax.all_gather(own_values, "rep", axis=0, tiled=True),
    )
    spat_query = select_heads(query, pick_spat)
    spat_mask = (
        jnp.einsum("hij,th->tij", block_mask.astype(jnp.float32), pick_spat.astype(jnp.float32))
        > 0.5
    )
    query_blocks = half_rows // BLK
    mask_rows = lax.dynamic_slice_in_dim(
        spat_mask, lax.axis_index("rep") * query_blocks, query_blocks, 1
    )
    scores = (
        jnp.einsum("qhd,khd->hqk", spat_query, spat_keys, preferred_element_type=jnp.float32)
        * score_scale
    )
    shaped = scores.reshape(spat_here, query_blocks, BLK, frame_blocks, BLK)
    shaped = jnp.where(mask_rows[:, :, None, :, None], shaped, MASKED_SCORE)
    weights = softmax_weights(shaped.reshape(spat_here, half_rows, frame_blocks * BLK))
    spat_out = jnp.einsum(
        "hqk,khd->qhd", weights, spat_values, preferred_element_type=jnp.float32
    ).astype(jnp.bfloat16)
    positions = jnp.arange(half_rows, dtype=jnp.int32)
    tile_ends = starts + tile_len
    tile_of = jnp.sum((positions[:, None] >= tile_ends[None, :]).astype(jnp.int32), axis=1)
    picked_start = jnp.sum(
        jnp.where(tile_of[:, None] == frame_range[None, :], starts[None, :], 0), axis=1
    )
    flat_index = tile_of * slot_count + positions - picked_start
    temp_out = returned.reshape(frame_count * slot_count, temp_here, HD)[flat_index]
    combined = spread_heads(spat_out, pick_spat) + spread_heads(temp_out, pick_temp)
    return combined.astype(jnp.bfloat16).reshape(half_rows, heads_here * HD)


EXP2_SCALE = HD ** -0.5 * math.log2(math.e)
HBM = pl.BlockSpec(memory_space=pltpu.HBM)
ANY = pl.BlockSpec(memory_space=pl.ANY)
SMEM = pl.BlockSpec(memory_space=pltpu.SMEM)
VMEM = pl.BlockSpec(memory_space=pltpu.VMEM)


def scores_of(rows, keys):
    return lax.dot_general(rows, keys, (((1,), (1,)), ((), ())), preferred_element_type=jnp.float32)


def attend(scores, values, ones=False):
    highest = scores[0]
    for more in scores[1:]:
        highest = jnp.maximum(highest, more)
    highest = highest.max(axis=-1, keepdims=True)
    out, total = 0.0, 0.0
    for group, group_values in zip(scores, values):
        raised = jnp.exp2((group - highest) * EXP2_SCALE)
        if ones:
            group_values = jnp.concatenate([group_values, jnp.ones_like(group_values)], axis=1)
        else:
            total = total + raised
        out = out + jnp.dot(raised.astype(jnp.bfloat16), group_values, preferred_element_type=jnp.float32)
    total = out[:, HD:] if ones else total.sum(axis=-1, keepdims=True)
    return (out[:, :HD] / total).astype(jnp.bfloat16)


def columns(index):
    return pl.ds(pl.multiple_of(index * HD, HD), HD)


def head_of(ids_ref, slot, heads_here):
    return lax.rem(ids_ref[slot], heads_here)


def pack_kernel(heads_here, parts, ids_hbm, query, key_proj, value, *rest):
    outs, ids_ref, sems = rest[: len(parts)], rest[-2], rest[-1]
    sources = {"q": query, "k": key_proj, "v": value}
    fetch = pltpu.make_async_copy(ids_hbm, ids_ref, sems.at[0])
    fetch.start()
    frame = lax.axis_index("frames")
    fetch.wait()
    copies = []
    for out, (mask, names) in zip(outs, parts):
        head = head_of(ids_ref, frame ^ mask, heads_here)
        for place, name in enumerate(names):
            copies.append(
                pltpu.make_async_copy(
                    sources[name].at[:, columns(head)],
                    out.at[:, place * HD : (place + 1) * HD],
                    sems.at[len(copies) + 1],
                )
            )
            copies[-1].start()
    for copy in copies:
        copy.wait()


def pack(ids, query, key_proj, value, parts, heads_here):
    rows = query.shape[0]
    count = sum(len(names) for _, names in parts)
    return pl.pallas_call(
        lambda *refs: pack_kernel(heads_here, parts, *refs),
        out_shape=[pltpu.VMEM((rows, len(names) * HD), query.dtype) for _, names in parts],
        in_specs=[HBM] * 4,
        out_specs=[VMEM] * len(parts),
        scratch_shapes=[pltpu.SMEM(ids.shape, jnp.int32), pltpu.SemaphoreType.DMA((count + 1,))],
        name="pack",
        compiler_params=pltpu.CompilerParams(vmem_limit_bytes=4 << 20),
        cost_estimate=pl.CostEstimate(flops=0, bytes_accessed=4 * count * rows * HD, transcendentals=0),
    )(*(pltpu.with_memory_space_constraint(array, pltpu.HBM) for array in (ids, query, key_proj, value)))


def spatial_kernel(heads_ref, mask_ref, query, key_own, key_other, value_own, value_other, out, bias_ref, asked, held, stage, arrive, leave):
    rows, count = query.shape[0], heads_ref.shape[0]
    own_blocks, frame_blocks = rows // BLK, mask_ref.shape[-1]
    coming = []
    for item in range(count):
        here = columns(heads_ref[item])
        for source, target in (
            (query, asked.at[item]),
            (key_own, held.at[item, 0, 0]),
            (value_own, held.at[item, 1, 0]),
            (key_other, held.at[item, 0, 1]),
            (value_other, held.at[item, 1, 1]),
        ):
            coming.append(pltpu.make_async_copy(source.at[:, here], target, arrive.at[len(coming)]))
            coming[-1].start()
    rep = lax.axis_index("rep")
    block = lax.broadcasted_iota(jnp.int32, (frame_blocks, 2 * rows), 1) // BLK
    block = lax.rem(block + rep * own_blocks, frame_blocks)
    spread = (block == lax.broadcasted_iota(jnp.int32, block.shape, 0)).astype(jnp.float32)
    for item in range(count):
        mask = mask_ref[heads_ref[item]].astype(jnp.float32)
        mask = jnp.where(rep == 0, mask[:own_blocks], mask[own_blocks:])
        seen = jnp.dot(mask, spread, preferred_element_type=jnp.float32)
        bias_ref[item] = jnp.where(seen > 0.5, 0.0, MASKED_SCORE)
    for copy in coming:
        copy.wait()
    going = []
    for item in range(count):
        bias = jnp.broadcast_to(bias_ref[item][:, None, :], (own_blocks, BLK, 2 * rows)).reshape(rows, 2 * rows)
        scores = [scores_of(asked[item], held[item, 0, half]) + bias[:, half * rows : (half + 1) * rows] for half in range(2)]
        stage[item] = attend(scores, [held[item, 1, half] for half in range(2)], ones=True)
        if (item + 1) % 4 == 0 or item + 1 == count:
            for sent in range(len(going), item + 1):
                going.append(pltpu.make_async_copy(stage.at[sent], out.at[:, columns(heads_ref[sent])], leave.at[sent]))
                going[-1].start()
    for copy in going:
        copy.wait()


def spatial(heads, mask, query, key_own, key_other, value_own, value_other):
    rows, width = query.shape
    count = heads.shape[0]
    query, key_own, value_own = (pltpu.with_memory_space_constraint(x, pltpu.HBM) for x in (query, key_own, value_own))
    return pl.pallas_call(
        spatial_kernel,
        out_shape=jax.ShapeDtypeStruct((rows, width), query.dtype),
        in_specs=[SMEM, VMEM, HBM, HBM, VMEM, HBM, VMEM],
        out_specs=HBM,
        scratch_shapes=[
            pltpu.VMEM((count, rows // BLK, 2 * rows), jnp.float32),
            pltpu.VMEM((count, rows, HD), query.dtype),
            pltpu.VMEM((count, 2, 2, rows, HD), query.dtype),
            pltpu.VMEM((count, rows, HD), query.dtype),
            pltpu.SemaphoreType.DMA((5 * count,)),
            pltpu.SemaphoreType.DMA((count,)),
        ],
        name="spatial",
        compiler_params=pltpu.CompilerParams(vmem_limit_bytes=16 << 20),
        cost_estimate=pl.CostEstimate(
            flops=8 * rows * rows * HD * count, bytes_accessed=12 * rows * HD * count, transcendentals=2 * rows * rows * count
        ),
    )(heads, mask, query, key_own, key_other, value_own, value_other)


def spatial_heads(ids, heads_here):
    head = jnp.arange(heads_here, dtype=jnp.int32)
    kept = jnp.all(lax.rem(ids, heads_here)[None, :] != head[:, None], axis=1)
    rank = jnp.sum((head[None, :] < head[:, None]) & kept[None, :], axis=1)
    place = jnp.arange(heads_here - ids.shape[0], dtype=jnp.int32)
    return jnp.sum(jnp.where(kept[None, :] & (rank[None, :] == place[:, None]), head[None, :], 0), axis=1)


def tile_bias_kernel(sizes_ref, out):
    rows = out.shape[0]
    down = lax.broadcasted_iota(jnp.int32, (rows, 1), 0)
    across = lax.broadcasted_iota(jnp.int32, (1, rows), 1)
    tile_down, tile_across, end = jnp.zeros_like(down), jnp.zeros_like(across), 0
    for tile in range(sizes_ref.shape[1]):
        end = end + sizes_ref[0, tile]
        tile_down = tile_down + (down >= end).astype(jnp.int32)
        tile_across = tile_across + (across >= end).astype(jnp.int32)
    out[...] = jnp.where(tile_down == tile_across, 0.0, MASKED_SCORE)


def tile_bias(sizes, rows):
    return pl.pallas_call(
        tile_bias_kernel,
        out_shape=jax.ShapeDtypeStruct((rows, rows), jnp.float32),
        in_specs=[SMEM],
        out_specs=VMEM,
        name="tile_bias",
        compiler_params=pltpu.CompilerParams(vmem_limit_bytes=4 << 20),
        cost_estimate=pl.CostEstimate(flops=rows * rows, bytes_accessed=4 * rows * rows, transcendentals=0),
    )(sizes)


def temporal_kernel(keys_at, queries, bias_ref, *refs):
    outs, pieces = refs[len(refs) - queries :], refs[: len(refs) - queries]
    query_refs, group_refs = pieces[:queries], pieces[queries:]
    bias = bias_ref[...]
    keys = [ref[:, at : at + HD] for ref, at in zip(group_refs, keys_at)]
    values = [ref[:, at + HD : at + 2 * HD] for ref, at in zip(group_refs, keys_at)]
    for query_ref, out in zip(query_refs, outs):
        rows = query_ref[:, :HD]
        out[...] = attend([scores_of(rows, group) + bias for group in keys], values)


def temporal(bias, queries, groups, keys_at):
    rows = bias.shape[0]
    work = len(queries) * len(groups) * rows * rows
    return pl.pallas_call(
        lambda *refs: temporal_kernel(keys_at, len(queries), *refs),
        out_shape=[jax.ShapeDtypeStruct((rows, HD), queries[0].dtype)] * len(queries),
        in_specs=[VMEM] * (1 + len(queries) + len(groups)),
        out_specs=[VMEM] * len(queries),
        name="temporal",
        compiler_params=pltpu.CompilerParams(vmem_limit_bytes=16 << 20),
        cost_estimate=pl.CostEstimate(
            flops=4 * work * HD, bytes_accessed=4 * (len(queries) + len(groups)) * rows * HD, transcendentals=work
        ),
    )(bias, *queries, *groups)


def merge_kernel(heads_here, masks, ids_ref, given, *rest):
    pieces, out, sems = rest[:-2], rest[-2], rest[-1]
    frame = lax.axis_index("frames")
    ids = lax.rem(ids_ref[...], heads_here).astype(jnp.float32)
    slot = lax.broadcasted_iota(jnp.int32, ids.shape, 1)
    copies = []
    for place, (mask, piece) in enumerate(zip(masks, pieces)):
        head = jnp.sum(jnp.where(slot == frame ^ mask, ids, 0.0)).astype(jnp.int32)
        copies.append(pltpu.make_async_copy(piece, out.at[:, columns(head)], sems.at[place]))
        copies[-1].start()
    for copy in copies:
        copy.wait()


def merge(ids, out, masks, pieces):
    rows, width = out.shape
    return pl.pallas_call(
        lambda *refs: merge_kernel(width // HD, masks, *refs),
        out_shape=jax.ShapeDtypeStruct(out.shape, out.dtype),
        in_specs=[VMEM, ANY] + [VMEM] * len(pieces),
        out_specs=ANY,
        scratch_shapes=[pltpu.SemaphoreType.DMA((len(pieces),))],
        input_output_aliases={1: 0},
        name="merge",
        compiler_params=pltpu.CompilerParams(vmem_limit_bytes=4 << 20),
        cost_estimate=pl.CostEstimate(flops=0, bytes_accessed=4 * len(pieces) * rows * HD, transcendentals=0),
    )(ids.reshape(1, -1), out, *pieces)


PLAN = ("s3", "s1", "k2", "d", "wk", "wv", "x", "q2", "a31", "b3", "b1", "a2", "b2", "a0")
NAMES = {"s": "qkv", "k": "kv", "q": "q"}


def local_by_head(query, key_proj, value, block_mask, tile_sizes, temporal_ids):
    frames = lax.axis_size("frames")
    heads_here = block_mask.shape[0]

    def exchange(array, mask):
        return lax.ppermute(array, "frames", [(i, i ^ mask) for i in range(frames)])

    sends = [step for step in PLAN if step[0] in NAMES]
    parts = [(int(step[1:]), NAMES[step[0]]) for step in sends] + [(0, "qkv")]
    packed = dict(zip(sends + ["own"], pack(temporal_ids, query, key_proj, value, parts, heads_here)))
    keys_sent, values_sent, *_ = lax.optimization_barrier((key_proj, value, *packed.values()))
    swapped = {"wk": keys_sent, "wv": values_sent}
    late = int([step for step in PLAN if step[0] == "b"][-1][1:])
    slot = jnp.arange(frames, dtype=jnp.int32) == lax.axis_index("frames") ^ late
    head = jnp.sum(jnp.where(slot, lax.rem(temporal_ids, heads_here), 0))
    heads, head = lax.optimization_barrier((spatial_heads(temporal_ids, heads_here), head))
    queries, groups, keys_at, attended, returned = {0: packed["own"]}, [packed["own"]], [HD], {}, {}
    for step in PLAN:
        kind, masks = step[0], [int(digit) for digit in step[1:] if digit.isdigit()]
        if kind in NAMES:
            arrived = exchange(packed[step], masks[0])
            if kind in "sq":
                queries[masks[0]] = arrived
            if kind in "sk":
                groups.append(arrived)
                keys_at.append(HD if kind == "s" else 0)
        elif kind == "w":
            swapped[step] = lax.ppermute(swapped[step], "rep", [(0, 1), (1, 0)])
        elif kind == "x":
            out = spatial(heads, block_mask, query, key_proj, swapped["wk"], value, swapped["wv"])
        elif kind == "d":
            bias = tile_bias(tile_sizes, query.shape[0])
        elif kind == "a":
            attended.update(zip(masks, temporal(bias, [queries[mask] for mask in masks], groups, keys_at)))
        elif kind == "b":
            returned[masks[0]] = exchange(attended[masks[0]], masks[0])
    returned[0] = attended[0]
    masks = [mask for mask in range(frames) if mask != late]
    out = merge(temporal_ids, out, masks, [returned[mask] for mask in masks])
    return lax.dynamic_update_slice(out, returned[late], (0, head * HD))


def local(query, key_proj, value, block_mask, tile_sizes, temporal_ids):
    frames, reps = lax.axis_size("frames"), lax.axis_size("rep")
    by_head = temporal_ids.shape[0] == frames == 4 and reps == 2
    form = local_by_head if by_head else local_by_tile
    return form(query, key_proj, value, block_mask, tile_sizes, temporal_ids)


def solution(mesh):
    in_specs = (
        P(("groups", "frames", "rep"), "heads"),
        P(("groups", "frames", "rep"), "heads"),
        P(("groups", "frames", "rep"), "heads"),
        P("heads", None, None),
        P("rep", None),
        P("heads"),
    )
    out_specs = P(("groups", "frames", "rep"), "heads")
    return jax.shard_map(local, mesh=mesh, in_specs=in_specs, out_specs=out_specs, check_vma=False)
```

```python
import math

import jax
import jax.numpy as jnp
from jax import lax
from jax.experimental import pallas as pl
from jax.experimental.pallas import tpu as pltpu
from jax.sharding import PartitionSpec as P


HD = 128
BLK = 64


MASKED_SCORE = -1e30


def softmax_weights(scores):
    highest = jnp.max(scores, axis=-1, keepdims=True)
    raised = jnp.exp(scores - highest)
    return (raised / jnp.sum(raised, axis=-1, keepdims=True)).astype(jnp.bfloat16)


def select_heads(token_rows, picker):
    head_grid = token_rows.reshape(token_rows.shape[0], -1, HD)
    chosen = jnp.einsum(
        "rhd,th->rtd", head_grid, picker.astype(jnp.bfloat16), preferred_element_type=jnp.float32
    )
    return chosen.astype(jnp.bfloat16)


def spread_heads(head_grid, picker):
    return jnp.einsum(
        "rtd,th->rhd", head_grid, picker.astype(jnp.bfloat16), preferred_element_type=jnp.float32
    )


def local_by_tile(query, key_proj, value, block_mask, tile_sizes, temporal_ids):
    half_rows = query.shape[0]
    heads_here = block_mask.shape[0]
    temp_here = temporal_ids.shape[0]
    spat_here = heads_here - temp_here
    frame_blocks = block_mask.shape[1]
    frame_count = lax.axis_size("frames")
    slot_count = 2 * half_rows // frame_count
    score_scale = HD ** (-0.5)
    local_ids = temporal_ids - lax.axis_index("heads") * heads_here
    head_range = jnp.arange(heads_here, dtype=jnp.int32)
    pick_temp = local_ids[:, None] == head_range[None, :]
    temp_flag = jnp.sum(pick_temp.astype(jnp.int32), axis=0)
    spat_rank = jnp.cumsum(1 - temp_flag) - 1
    pick_spat = (spat_rank[None, :] == jnp.arange(spat_here, dtype=jnp.int32)[:, None]) & (
        temp_flag[None, :] == 0
    )
    tile_len = tile_sizes[0]
    starts = jnp.cumsum(tile_len) - tile_len
    slot_index = jnp.arange(slot_count, dtype=jnp.int32)
    source_rows = jnp.minimum(starts[:, None] + slot_index[None, :], half_rows - 1)
    frame_range = jnp.arange(frame_count, dtype=jnp.int32)
    own_len = jnp.sum(jnp.where(frame_range == lax.axis_index("frames"), tile_len, 0))
    key_live = jnp.tile(slot_index < own_len, frame_count)
    send_query = select_heads(query, pick_temp)[source_rows]
    send_keys = select_heads(key_proj, pick_temp)[source_rows]
    send_values = select_heads(value, pick_temp)[source_rows]
    tile_query = lax.all_to_all(send_query, "frames", split_axis=0, concat_axis=0, tiled=True)
    tile_keys = lax.all_to_all(send_keys, "frames", split_axis=0, concat_axis=0, tiled=True)
    tile_values = lax.all_to_all(send_values, "frames", split_axis=0, concat_axis=0, tiled=True)
    item_count = tile_query.shape[2]
    flat_query = tile_query.reshape(frame_count * slot_count, item_count, HD)
    flat_keys = tile_keys.reshape(frame_count * slot_count, item_count, HD)
    flat_values = tile_values.reshape(frame_count * slot_count, item_count, HD)
    scores = (
        jnp.einsum("qhd,khd->hqk", flat_query, flat_keys, preferred_element_type=jnp.float32)
        * score_scale
    )
    scores = jnp.where(key_live[None, None, :], scores, MASKED_SCORE)
    weights = softmax_weights(scores)
    tile_out = jnp.einsum(
        "hqk,khd->qhd", weights, flat_values, preferred_element_type=jnp.float32
    ).astype(jnp.bfloat16)
    returned = lax.all_to_all(
        tile_out.reshape(frame_count, slot_count, item_count, HD),
        "frames",
        split_axis=0,
        concat_axis=0,
        tiled=True,
    )
    own_keys = select_heads(key_proj, pick_spat)
    own_values = select_heads(value, pick_spat)
    spat_keys, spat_values = (
        lax.all_gather(own_keys, "rep", axis=0, tiled=True),
        lax.all_gather(own_values, "rep", axis=0, tiled=True),
    )
    spat_query = select_heads(query, pick_spat)
    spat_mask = (
        jnp.einsum("hij,th->tij", block_mask.astype(jnp.float32), pick_spat.astype(jnp.float32))
        > 0.5
    )
    query_blocks = half_rows // BLK
    mask_rows = lax.dynamic_slice_in_dim(
        spat_mask, lax.axis_index("rep") * query_blocks, query_blocks, 1
    )
    scores = (
        jnp.einsum("qhd,khd->hqk", spat_query, spat_keys, preferred_element_type=jnp.float32)
        * score_scale
    )
    shaped = scores.reshape(spat_here, query_blocks, BLK, frame_blocks, BLK)
    shaped = jnp.where(mask_rows[:, :, None, :, None], shaped, MASKED_SCORE)
    weights = softmax_weights(shaped.reshape(spat_here, half_rows, frame_blocks * BLK))
    spat_out = jnp.einsum(
        "hqk,khd->qhd", weights, spat_values, preferred_element_type=jnp.float32
    ).astype(jnp.bfloat16)
    positions = jnp.arange(half_rows, dtype=jnp.int32)
    tile_ends = starts + tile_len
    tile_of = jnp.sum((positions[:, None] >= tile_ends[None, :]).astype(jnp.int32), axis=1)
    picked_start = jnp.sum(
        jnp.where(tile_of[:, None] == frame_range[None, :], starts[None, :], 0), axis=1
    )
    flat_index = tile_of * slot_count + positions - picked_start
    temp_out = returned.reshape(frame_count * slot_count, temp_here, HD)[flat_index]
    combined = spread_heads(spat_out, pick_spat) + spread_heads(temp_out, pick_temp)
    return combined.astype(jnp.bfloat16).reshape(half_rows, heads_here * HD)


EXP2_SCALE = HD ** -0.5 * math.log2(math.e)
HBM = pl.BlockSpec(memory_space=pltpu.HBM)
ANY = pl.BlockSpec(memory_space=pl.ANY)
SMEM = pl.BlockSpec(memory_space=pltpu.SMEM)
VMEM = pl.BlockSpec(memory_space=pltpu.VMEM)


def scores_of(rows, keys):
    return lax.dot_general(rows, keys, (((1,), (1,)), ((), ())), preferred_element_type=jnp.float32)


def attend(scores, values, ones=False):
    highest = scores[0]
    for more in scores[1:]:
        highest = jnp.maximum(highest, more)
    highest = highest.max(axis=-1, keepdims=True)
    out, total = 0.0, 0.0
    for group, group_values in zip(scores, values):
        raised = jnp.exp2((group - highest) * EXP2_SCALE)
        if ones:
            group_values = jnp.concatenate([group_values, jnp.ones_like(group_values)], axis=1)
        else:
            total = total + raised
        out = out + jnp.dot(raised.astype(jnp.bfloat16), group_values, preferred_element_type=jnp.float32)
    total = out[:, HD:] if ones else total.sum(axis=-1, keepdims=True)
    return (out[:, :HD] / total).astype(jnp.bfloat16)


def columns(index):
    return pl.ds(pl.multiple_of(index * HD, HD), HD)


def head_of(ids_ref, slot, heads_here):
    return lax.rem(ids_ref[slot], heads_here)


def pack_kernel(heads_here, parts, ids_hbm, query, key_proj, value, *rest):
    outs, ids_ref, sems = rest[: len(parts)], rest[-2], rest[-1]
    sources = {"q": query, "k": key_proj, "v": value}
    fetch = pltpu.make_async_copy(ids_hbm, ids_ref, sems.at[0])
    fetch.start()
    frame = lax.axis_index("frames")
    fetch.wait()
    copies = []
    for out, (mask, names) in zip(outs, parts):
        head = head_of(ids_ref, frame ^ mask, heads_here)
        for place, name in enumerate(names):
            copies.append(
                pltpu.make_async_copy(
                    sources[name].at[:, columns(head)],
                    out.at[:, place * HD : (place + 1) * HD],
                    sems.at[len(copies) + 1],
                )
            )
            copies[-1].start()
    for copy in copies:
        copy.wait()


def pack(ids, query, key_proj, value, parts, heads_here):
    rows = query.shape[0]
    count = sum(len(names) for _, names in parts)
    return pl.pallas_call(
        lambda *refs: pack_kernel(heads_here, parts, *refs),
        out_shape=[pltpu.VMEM((rows, len(names) * HD), query.dtype) for _, names in parts],
        in_specs=[HBM] * 4,
        out_specs=[VMEM] * len(parts),
        scratch_shapes=[pltpu.SMEM(ids.shape, jnp.int32), pltpu.SemaphoreType.DMA((count + 1,))],
        name="pack",
        compiler_params=pltpu.CompilerParams(vmem_limit_bytes=4 << 20),
        cost_estimate=pl.CostEstimate(flops=0, bytes_accessed=4 * count * rows * HD, transcendentals=0),
    )(*(pltpu.with_memory_space_constraint(array, pltpu.HBM) for array in (ids, query, key_proj, value)))


def spatial_kernel(heads_ref, mask_ref, query, key_own, key_other, value_own, value_other, out, bias_ref, asked, held, stage, arrive, leave):
    rows, count = query.shape[0], heads_ref.shape[0]
    own_blocks, frame_blocks = rows // BLK, mask_ref.shape[-1]
    coming = []
    for item in range(count):
        here = columns(heads_ref[item])
        for source, target in (
            (query, asked.at[item]),
            (key_own, held.at[item, 0, 0]),
            (value_own, held.at[item, 1, 0]),
            (key_other, held.at[item, 0, 1]),
            (value_other, held.at[item, 1, 1]),
        ):
            coming.append(pltpu.make_async_copy(source.at[:, here], target, arrive.at[len(coming)]))
            coming[-1].start()
    rep = lax.axis_index("rep")
    block = lax.broadcasted_iota(jnp.int32, (frame_blocks, 2 * rows), 1) // BLK
    block = lax.rem(block + rep * own_blocks, frame_blocks)
    spread = (block == lax.broadcasted_iota(jnp.int32, block.shape, 0)).astype(jnp.float32)
    for item in range(count):
        mask = mask_ref[heads_ref[item]].astype(jnp.float32)
        mask = jnp.where(rep == 0, mask[:own_blocks], mask[own_blocks:])
        seen = jnp.dot(mask, spread, preferred_element_type=jnp.float32)
        bias_ref[item] = jnp.where(seen > 0.5, 0.0, MASKED_SCORE)
    for copy in coming:
        copy.wait()
    going = []
    for item in range(count):
        bias = jnp.broadcast_to(bias_ref[item][:, None, :], (own_blocks, BLK, 2 * rows)).reshape(rows, 2 * rows)
        scores = [scores_of(asked[item], held[item, 0, half]) + bias[:, half * rows : (half + 1) * rows] for half in range(2)]
        stage[item] = attend(scores, [held[item, 1, half] for half in range(2)], ones=True)
        if (item + 1) % 4 == 0 or item + 1 == count:
            for sent in range(len(going), item + 1):
                going.append(pltpu.make_async_copy(stage.at[sent], out.at[:, columns(heads_ref[sent])], leave.at[sent]))
                going[-1].start()
    for copy in going:
        copy.wait()


def spatial(heads, mask, query, key_own, key_other, value_own, value_other):
    rows, width = query.shape
    count = heads.shape[0]
    query, key_own, value_own = (pltpu.with_memory_space_constraint(x, pltpu.HBM) for x in (query, key_own, value_own))
    return pl.pallas_call(
        spatial_kernel,
        out_shape=jax.ShapeDtypeStruct((rows, width), query.dtype),
        in_specs=[SMEM, VMEM, HBM, HBM, VMEM, HBM, VMEM],
        out_specs=HBM,
        scratch_shapes=[
            pltpu.VMEM((count, rows // BLK, 2 * rows), jnp.float32),
            pltpu.VMEM((count, rows, HD), query.dtype),
            pltpu.VMEM((count, 2, 2, rows, HD), query.dtype),
            pltpu.VMEM((count, rows, HD), query.dtype),
            pltpu.SemaphoreType.DMA((5 * count,)),
            pltpu.SemaphoreType.DMA((count,)),
        ],
        name="spatial",
        compiler_params=pltpu.CompilerParams(vmem_limit_bytes=16 << 20),
        cost_estimate=pl.CostEstimate(
            flops=8 * rows * rows * HD * count, bytes_accessed=12 * rows * HD * count, transcendentals=2 * rows * rows * count
        ),
    )(heads, mask, query, key_own, key_other, value_own, value_other)


def spatial_heads(ids, heads_here):
    head = jnp.arange(heads_here, dtype=jnp.int32)
    kept = jnp.all(lax.rem(ids, heads_here)[None, :] != head[:, None], axis=1)
    rank = jnp.sum((head[None, :] < head[:, None]) & kept[None, :], axis=1)
    place = jnp.arange(heads_here - ids.shape[0], dtype=jnp.int32)
    return jnp.sum(jnp.where(kept[None, :] & (rank[None, :] == place[:, None]), head[None, :], 0), axis=1)


def tile_bias_kernel(sizes_ref, out):
    rows = out.shape[0]
    down = lax.broadcasted_iota(jnp.int32, (rows, 1), 0)
    across = lax.broadcasted_iota(jnp.int32, (1, rows), 1)
    tile_down, tile_across, end = jnp.zeros_like(down), jnp.zeros_like(across), 0
    for tile in range(sizes_ref.shape[1]):
        end = end + sizes_ref[0, tile]
        tile_down = tile_down + (down >= end).astype(jnp.int32)
        tile_across = tile_across + (across >= end).astype(jnp.int32)
    out[...] = jnp.where(tile_down == tile_across, 0.0, MASKED_SCORE)


def tile_bias(sizes, rows):
    return pl.pallas_call(
        tile_bias_kernel,
        out_shape=jax.ShapeDtypeStruct((rows, rows), jnp.float32),
        in_specs=[SMEM],
        out_specs=VMEM,
        name="tile_bias",
        compiler_params=pltpu.CompilerParams(vmem_limit_bytes=4 << 20),
        cost_estimate=pl.CostEstimate(flops=rows * rows, bytes_accessed=4 * rows * rows, transcendentals=0),
    )(sizes)


def temporal_kernel(keys_at, queries, bias_ref, *refs):
    outs, pieces = refs[len(refs) - queries :], refs[: len(refs) - queries]
    query_refs, group_refs = pieces[:queries], pieces[queries:]
    bias = bias_ref[...]
    keys = [ref[:, at : at + HD] for ref, at in zip(group_refs, keys_at)]
    values = [ref[:, at + HD : at + 2 * HD] for ref, at in zip(group_refs, keys_at)]
    for query_ref, out in zip(query_refs, outs):
        rows = query_ref[:, :HD]
        out[...] = attend([scores_of(rows, group) + bias for group in keys], values)


def temporal(bias, queries, groups, keys_at):
    rows = bias.shape[0]
    work = len(queries) * len(groups) * rows * rows
    return pl.pallas_call(
        lambda *refs: temporal_kernel(keys_at, len(queries), *refs),
        out_shape=[jax.ShapeDtypeStruct((rows, HD), queries[0].dtype)] * len(queries),
        in_specs=[VMEM] * (1 + len(queries) + len(groups)),
        out_specs=[VMEM] * len(queries),
        name="temporal",
        compiler_params=pltpu.CompilerParams(vmem_limit_bytes=16 << 20),
        cost_estimate=pl.CostEstimate(
            flops=4 * work * HD, bytes_accessed=4 * (len(queries) + len(groups)) * rows * HD, transcendentals=work
        ),
    )(bias, *queries, *groups)


def merge_kernel(heads_here, masks, ids_ref, given, *rest):
    pieces, out, sems = rest[:-2], rest[-2], rest[-1]
    frame = lax.axis_index("frames")
    ids = lax.rem(ids_ref[...], heads_here).astype(jnp.float32)
    slot = lax.broadcasted_iota(jnp.int32, ids.shape, 1)
    copies = []
    for place, (mask, piece) in enumerate(zip(masks, pieces)):
        head = jnp.sum(jnp.where(slot == frame ^ mask, ids, 0.0)).astype(jnp.int32)
        copies.append(pltpu.make_async_copy(piece, out.at[:, columns(head)], sems.at[place]))
        copies[-1].start()
    for copy in copies:
        copy.wait()


def merge(ids, out, masks, pieces):
    rows, width = out.shape
    return pl.pallas_call(
        lambda *refs: merge_kernel(width // HD, masks, *refs),
        out_shape=jax.ShapeDtypeStruct(out.shape, out.dtype),
        in_specs=[VMEM, ANY] + [VMEM] * len(pieces),
        out_specs=ANY,
        scratch_shapes=[pltpu.SemaphoreType.DMA((len(pieces),))],
        input_output_aliases={1: 0},
        name="merge",
        compiler_params=pltpu.CompilerParams(vmem_limit_bytes=4 << 20),
        cost_estimate=pl.CostEstimate(flops=0, bytes_accessed=4 * len(pieces) * rows * HD, transcendentals=0),
    )(ids.reshape(1, -1), out, *pieces)


PLAN = ("s3", "s1", "k2", "d", "wk", "wv", "p", "x", "q2", "a31", "b3", "b1", "a2", "b2", "a0")
NAMES = {"s": "qkv", "k": "kv", "q": "q"}


def local_by_head(query, key_proj, value, block_mask, tile_sizes, temporal_ids):
    frames = lax.axis_size("frames")
    heads_here = block_mask.shape[0]

    def exchange(array, mask):
        return lax.ppermute(array, "frames", [(i, i ^ mask) for i in range(frames)])

    sends = [step for step in PLAN if step[0] in NAMES]
    early = [step for step in sends if step[0] != "q"]
    rest = [step for step in sends if step[0] == "q"] + ["own"]

    def packed_for(steps, *operands):
        parts = [(0, "qkv") if step == "own" else (int(step[1:]), NAMES[step[0]]) for step in steps]
        return dict(zip(steps, pack(temporal_ids, *operands, parts, heads_here)))

    packed = packed_for(early, query, key_proj, value)
    keys_sent, values_sent, *_ = lax.optimization_barrier((key_proj, value, *packed.values()))
    swapped = {"wk": keys_sent, "wv": values_sent}
    late = int([step for step in PLAN if step[0] == "b"][-1][1:])
    slot = jnp.arange(frames, dtype=jnp.int32) == lax.axis_index("frames") ^ late
    head = jnp.sum(jnp.where(slot, lax.rem(temporal_ids, heads_here), 0))
    heads, head = lax.optimization_barrier((spatial_heads(temporal_ids, heads_here), head))
    queries, groups, keys_at, attended, returned = {}, [], [], {}, {}
    for step in PLAN:
        kind, masks = step[0], [int(digit) for digit in step[1:] if digit.isdigit()]
        if kind in NAMES:
            arrived = exchange(packed[step], masks[0])
            if kind in "sq":
                queries[masks[0]] = arrived
            if kind in "sk":
                groups.append(arrived)
                keys_at.append(HD if kind == "s" else 0)
        elif kind == "w":
            swapped[step] = lax.ppermute(swapped[step], "rep", [(0, 1), (1, 0)])
        elif kind == "x":
            out = spatial(heads, block_mask, query, key_proj, swapped["wk"], value, swapped["wv"])
        elif kind == "p":
            late_query, *_ = lax.optimization_barrier((query, *packed.values()))
            packed.update(packed_for(rest, late_query, key_proj, value))
            queries[0] = packed["own"]
            groups.append(packed["own"])
            keys_at.append(HD)
        elif kind == "d":
            bias = tile_bias(tile_sizes, query.shape[0])
        elif kind == "a":
            attended.update(zip(masks, temporal(bias, [queries[mask] for mask in masks], groups, keys_at)))
        elif kind == "b":
            returned[masks[0]] = exchange(attended[masks[0]], masks[0])
    returned[0] = attended[0]
    masks = [mask for mask in range(frames) if mask != late]
    out = merge(temporal_ids, out, masks, [returned[mask] for mask in masks])
    return lax.dynamic_update_slice(out, returned[late], (0, head * HD))


def local(query, key_proj, value, block_mask, tile_sizes, temporal_ids):
    frames, reps = lax.axis_size("frames"), lax.axis_size("rep")
    by_head = temporal_ids.shape[0] == frames == 4 and reps == 2
    form = local_by_head if by_head else local_by_tile
    return form(query, key_proj, value, block_mask, tile_sizes, temporal_ids)


def solution(mesh):
    in_specs = (
        P(("groups", "frames", "rep"), "heads"),
        P(("groups", "frames", "rep"), "heads"),
        P(("groups", "frames", "rep"), "heads"),
        P("heads", None, None),
        P("rep", None),
        P("heads"),
    )
    out_specs = P(("groups", "frames", "rep"), "heads")
    return jax.shard_map(local, mesh=mesh, in_specs=in_specs, out_specs=out_specs, check_vma=False)
```
